128 devices in a mesh: sx: 8 (over z, core), sy: 8 (over x_lo, y), rep: 2 (over x_hi).
Axes of the slice: x: 4 (x_hi: 2, x_lo: 2; x = x_hi * 2 + x_lo), y: 4, z: 4, core: 2. Of those that a mesh axis runs over, the one named last changes fastest.
Arguments:
- volume: bfloat16 [2, 32, 16, 128, 256], P('rep', None, 'sx', 'sy'), may hold values from -6 to 6
- first_kernel: bfloat16 [64, 32, 3, 3, 3], replicated, may hold values from -0.21875 to 0.21875
- first_bias: float32 [64], replicated, may hold values from -3 to 3
- second_kernel: bfloat16 [128, 64, 3, 3, 3], P('sy'), may hold values from -0.15625 to 0.15625
- second_bias: float32 [128], P('sy'), may hold values from -3 to 3
- cotangent: bfloat16 [2, 128, 8, 64, 128], P('rep', 'sy', 'sx'), may hold values from -6 to 6
Outputs:
- second_out: float32 [2, 128, 8, 64, 128], P('rep', 'sy', 'sx')
- grad_first_kernel: float32 [64, 32, 3, 3, 3], replicated
- grad_first_bias: float32 [64], replicated
- grad_second_kernel: float32 [128, 64, 3, 3, 3], P('sy')
- grad_second_bias: float32 [128], P('sy')
The draws below stay inside these ranges and needn't reach their ends.
All inputs are finite; a program needn't handle non-finite values.
Results may differ from the reference program's by a relative error of at most 0.0045.
Values may be sent and summed in bfloat16 or wider, within the bound.
A program may use at most 128 MiB of HBM per device.

```python
import jax
import jax.numpy as jnp
from jax import lax

CIN = 32
C1 = 64
C2 = 128
CZ = 256
BATCH = 2
NX = 16
NY = 128
NX2 = 8
NY2 = 64
CZ2 = 128


def block_levels(stream_key, dims, cuts, smallest, top_value):
    def one(position, shards_of):
        steps = jax.random.uniform(jax.random.fold_in(jax.random.fold_in(stream_key, 6), position), (shards_of,), jnp.float32, smallest / len(cuts), top_value / len(cuts))
        return jnp.repeat(jnp.exp(steps), dims[position] // shards_of).reshape((-1,) + (1,) * (len(dims) - position - 1))

    factor_of = one(*cuts[0])
    for cut in cuts[1:]:
        factor_of = factor_of * one(*cut)
    return factor_of


def scatter_about(stream_key, extent, scale, bound, cuts=(), held_as=jnp.bfloat16):
    factor_of = block_levels(stream_key, extent, cuts, -0.22, 0.18) if cuts else 1.0
    entries = jax.random.normal(stream_key, extent, jnp.float32) * scale * factor_of
    return jnp.minimum(jnp.maximum(entries, -bound), bound).astype(held_as)


def setup_inputs(seed: int = 0) -> dict:
    streams_of = jax.random.split(jax.random.key(seed), 7)
    return {
        "volume": scatter_about(streams_of[0], (BATCH, CIN, NX, NY, CZ), 1.0, 6.0, ((0, 2), (2, 8), (3, 8))),
        "first_kernel": scatter_about(streams_of[1], (C1, CIN, 3, 3, 3), (CIN * 27) ** -0.5, 0.21875),
        "first_bias": scatter_about(streams_of[2], (C1,), 0.5, 3.0, (), jnp.float32),
        "second_kernel": scatter_about(streams_of[3], (C2, C1, 3, 3, 3), (C1 * 27) ** -0.5, 0.15625, ((0, 8),)),
        "second_bias": scatter_about(streams_of[4], (C2,), 0.5, 3.0, ((0, 8),), jnp.float32),
        "cotangent": scatter_about(streams_of[5], (BATCH, C2, NX2, NY2, CZ2), 1.0, 6.0, ((0, 2), (1, 8), (2, 8))),
    }


def convolve(field, kernel):
    return lax.conv_general_dilated(field[None], kernel, (1, 1, 1), 'SAME', dimension_numbers=('NCDHW', 'OIDHW', 'NCDHW'), preferred_element_type=jnp.float32)[0]

def weight_terms(cotan, source):
    cells_x, cells_y, cells_z = (cotan.shape[1], cotan.shape[2], cotan.shape[3])
    padded = jnp.pad(source.astype(jnp.float32), ((0, 0), (1, 1), (1, 1), (1, 1)))
    grads = cotan.astype(jnp.float32)
    terms = []
    for i in range(3):
        for j in range(3):
            for k in range(3):
                piece = padded[:, i:i + cells_x, j:j + cells_y, k:k + cells_z]
                terms.append(jnp.einsum('oxyz,cxyz->oc', grads, piece, precision=lax.Precision.HIGHEST))
    stacked = jnp.stack(terms).reshape(3, 3, 3, grads.shape[0], source.shape[0])
    return stacked.transpose(3, 4, 0, 1, 2)

def pool_mean(field):
    chans, cells_x, cells_y, cells_z = field.shape
    blocks = field.astype(jnp.float32).reshape(chans, cells_x // 2, 2, cells_y // 2, 2, cells_z // 2, 2)
    return lax.optimization_barrier(jnp.mean(blocks, axis=(2, 4, 6)))

def reference(volume, first_kernel, first_bias, second_kernel, second_bias, cotangent):
    scale = 1.0 / jnp.sqrt(jnp.float32(BATCH * NX2 * NY2 * CZ2))
    flipped = second_kernel.transpose(1, 0, 2, 3, 4)[:, :, ::-1, ::-1, ::-1]
    outs = []
    grad_w1 = jnp.zeros((C1, CIN, 3, 3, 3), jnp.float32)
    grad_b1 = jnp.zeros((C1,), jnp.float32)
    grad_w2 = jnp.zeros((C2, C1, 3, 3, 3), jnp.float32)
    grad_b2 = jnp.zeros((C2,), jnp.float32)
    for sample in range(BATCH):
        source = volume[sample]
        pre = convolve(source, first_kernel) + first_bias[:, None, None, None]
        act = jnp.where(pre > 0, pre, 0.3 * pre)
        pooled = pool_mean(act).astype(jnp.bfloat16)
        second = convolve(pooled, second_kernel) + second_bias[:, None, None, None]
        outs.append(second.astype(jnp.float32))
        cotan = cotangent[sample]
        grad_w2 = grad_w2 + weight_terms(cotan, pooled)
        grad_b2 = grad_b2 + lax.optimization_barrier(jnp.sum(cotan.astype(jnp.float32), axis=(1, 2, 3)))
        back = convolve(cotan, flipped)
        spread = jnp.repeat(jnp.repeat(jnp.repeat(back, 2, axis=1), 2, axis=2), 2, axis=3)
        grad_pre = (spread * 0.125 * jnp.where(pre > 0, 1.0, 0.3)).astype(jnp.bfloat16)
        grad_w1 = grad_w1 + weight_terms(grad_pre, source)
        grad_b1 = grad_b1 + lax.optimization_barrier(jnp.sum(grad_pre.astype(jnp.float32), axis=(1, 2, 3)))
    second_out = jnp.stack(outs)
    return (second_out, scale * grad_w1, scale * grad_b1, scale * grad_w2, scale * grad_b2)
```

```python
import math

import jax
import jax.numpy as jnp
from jax import lax
from jax.experimental import pallas as pl
from jax.experimental.pallas import tpu as pltpu
from jax.sharding import PartitionSpec as P

MESH = pl.DeviceIdType.MESH
BF16 = jnp.bfloat16
F32 = jnp.float32
NEIGHBOURS = [(dx, dy) for dx in (-1, 0, 1) for dy in (-1, 0, 1) if (dx, dy) != (0, 0)]
VMEM = pl.BlockSpec(memory_space=pltpu.VMEM)
LIMIT = 60 * 1024 * 1024


def place():
    return lax.axis_index("sx"), lax.axis_index("sy"), lax.axis_index("rep")


def remote(src, dst, send, recv, device):
    return pltpu.make_async_remote_copy(
        src_ref=src, dst_ref=dst, send_sem=send, recv_sem=recv, device_id=device, device_id_type=MESH
    )


def greet(devices):
    barrier = pltpu.get_barrier_semaphore()
    for device in devices:
        pl.semaphore_signal(barrier, inc=1, device_id=device, device_id_type=MESH)
    pl.semaphore_wait(barrier, len(devices))


def halo_copies(src, dst, send, recv):
    sx, sy, rep = place()
    cells_x, cells_y = src.shape[0], src.shape[1]
    rim_x, rim_y = cells_x + 1, cells_y + 1
    copies = []
    for k, (dx, dy) in enumerate(NEIGHBOURS):
        from_x = {1: pl.ds(cells_x - 1, 1), -1: pl.ds(0, 1), 0: pl.ds(0, cells_x)}[dx]
        from_y = {1: pl.ds(cells_y - 1, 1), -1: pl.ds(0, 1), 0: pl.ds(0, cells_y)}[dy]
        to_x = {1: pl.ds(0, 1), -1: pl.ds(rim_x, 1), 0: pl.ds(1, cells_x)}[dx]
        to_y = {1: pl.ds(0, 1), -1: pl.ds(rim_y, 1), 0: pl.ds(1, cells_y)}[dy]
        device = ((sx + (dx + 8)) % 8, (sy + (dy + 8)) % 8, rep)
        copies.append(remote(src.at[from_x, from_y], dst.at[to_x, to_y], send.at[k], recv.at[k], device))
    return copies


def clear_rim(dst):
    sx, sy, _ = place()
    rim_x, rim_y = dst.shape[0] - 1, dst.shape[1] - 1

    @pl.when(sx == 0)
    def _():
        dst[0] = jnp.zeros(dst.shape[1:], dst.dtype)

    @pl.when(sx == 7)
    def _():
        dst[rim_x] = jnp.zeros(dst.shape[1:], dst.dtype)

    @pl.when(sy == 0)
    def _():
        dst[:, 0] = jnp.zeros((dst.shape[0],) + dst.shape[2:], dst.dtype)

    @pl.when(sy == 7)
    def _():
        dst[:, rim_y] = jnp.zeros((dst.shape[0],) + dst.shape[2:], dst.dtype)


def spread_kernel(vol, cot, wf, wb, vol_pad, cot_pad, wf_all, wb_all, local_sem, vs, vr, cs, cr, fs, fr, ws, wr):
    sx, sy, rep = place()
    left, right = (sx + 7) % 8, (sx + 1) % 8
    greet(
        [((sx + (dx + 8)) % 8, (sy + (dy + 8)) % 8, rep) for dx in (-1, 1) for dy in (-1, 0, 1)]
        + [(sx, (sy + d) % 8, rep) for d in range(1, 8)]
    )
    volume_copies = halo_copies(vol, vol_pad, vs, vr)
    for copy in volume_copies:
        copy.start()
    mine = pl.ds(pl.multiple_of(16 * sy, 16), 16)
    exchange = []
    for d in range(1, 8):
        peer = (sy + d) % 8
        copy = remote(
            cot.at[pl.ds(8 * peer, 10)], cot_pad.at[1, :, mine, :], cs.at[d], cr.at[d], (sx, peer, rep)
        )
        copy.start()
        exchange.append(copy)
    own_cot = cot.at[pl.ds(8 * sy, 10)]
    locals_ = [
        pltpu.make_async_copy(vol, vol_pad.at[pl.ds(1, 2), pl.ds(1, 16)], local_sem.at[0]),
        pltpu.make_async_copy(own_cot, cot_pad.at[1, :, mine, :], local_sem.at[1]),
        pltpu.make_async_copy(wf, wf_all.at[:, mine, :], local_sem.at[2]),
        pltpu.make_async_copy(wb, wb_all.at[:, mine, :], local_sem.at[3]),
    ]
    for copy in locals_:
        copy.start()
    weights = []
    for d in range(1, 8):
        peer = (sx, (sy + d) % 8, rep)
        weights.append(remote(wf, wf_all.at[:, mine, :], ws.at[d], wr.at[d], peer))
        weights.append(remote(wb, wb_all.at[:, mine, :], ws.at[8 + d], wr.at[8 + d], peer))
    for copy in weights:
        copy.start()
    forwards = []
    for d in range(8):
        rows = pl.ds(pl.multiple_of(16 * ((sy + (8 - d)) % 8), 16), 16)
        if d:
            exchange[d - 1].wait_recv()
            source = cot_pad.at[1, :, rows, :]
        else:
            source = own_cot
        forwards.append(remote(source, cot_pad.at[2, :, rows, :], fs.at[d], fr.at[d], (left, sy, rep)))
        forwards.append(remote(source, cot_pad.at[0, :, rows, :], fs.at[8 + d], fr.at[8 + d], (right, sy, rep)))
        forwards[-2].start()
        forwards[-1].start()
    for copy in locals_ + volume_copies + weights + forwards:
        copy.wait()
    for copy in exchange:
        copy.wait_send()
    clear_rim(vol_pad)

    @pl.when(sx == 0)
    def _():
        cot_pad[0] = jnp.zeros(cot_pad.shape[1:], BF16)

    @pl.when(sx == 7)
    def _():
        cot_pad[2] = jnp.zeros(cot_pad.shape[1:], BF16)


def halo_kernel(src, dst, local_sem, send, recv):
    sx, sy, rep = place()
    greet([((sx + (dx + 8)) % 8, (sy + (dy + 8)) % 8, rep) for dx, dy in NEIGHBOURS])
    copies = halo_copies(src, dst, send, recv)
    for copy in copies:
        copy.start()
    own = pltpu.make_async_copy(src, dst.at[pl.ds(1, 1), pl.ds(1, 8)], local_sem)
    own.start()
    own.wait()
    for copy in copies:
        copy.wait()
    clear_rim(dst)


def shifted(block, step):
    width = block.shape[-1]
    lanes = lax.broadcasted_iota(jnp.int32, block.shape, block.ndim - 1)
    if step == 1:
        return jnp.where(lanes == width - 1, 0.0, pltpu.roll(block, width - 1, block.ndim - 1))
    return jnp.where(lanes == 0, 0.0, pltpu.roll(block, 1, block.ndim - 1))


def combine(stacked, chans):
    return (
        stacked[chans : 2 * chans] + shifted(stacked[:chans], -1) + shifted(stacked[2 * chans :], 1)
    )


def split(block):
    high = block.astype(BF16)
    return high, (block - high.astype(F32)).astype(BF16)


def pairs_of(shape, across):
    rows = lax.broadcasted_iota(jnp.int32, shape, 0)
    columns = lax.broadcasted_iota(jnp.int32, shape, 1)
    hit = (rows // 2 == columns) if across == 0 else (columns // 2 == rows)
    return jnp.where(hit, 1.0, 0.0).astype(BF16)


def first_kernel_body(vol_pad, w1, b1, pooled, mask):
    gather = pairs_of((256, 128), 0)

    def row(y2, carry):
        total = jnp.zeros((64, 256), F32)
        for x in range(2):
            for j in range(2):
                y = 2 * y2 + j
                cells = vol_pad[pl.ds(x, 3), pl.ds(y, 3)].reshape(288, 256)
                pre = combine(jnp.dot(w1[...], cells, preferred_element_type=F32), 64) + b1[...]
                mask[x, y] = jnp.where(pre > 0, 1.0, 0.0).astype(BF16)
                total = total + jnp.where(pre > 0, pre, 0.3 * pre)
        high, low = split(total)
        summed = jnp.dot(high, gather, preferred_element_type=F32) + jnp.dot(
            low, gather, preferred_element_type=F32
        )
        pooled[0, y2] = (summed * 0.125).astype(BF16)
        return carry

    lax.fori_loop(0, 8, row, 0)


def second_kernel_body(vol_pad, cot_pad, wf, wbt, pool_pad, mask, second, gw2, gw1):
    spread = pairs_of((128, 256), 1)
    gw1[...] = jnp.zeros_like(gw1)
    gw2[...] = jnp.zeros_like(gw2)

    def two_rows(ref, y, chans):
        return jnp.concatenate(
            [ref[:, pl.ds(y + j, 3)].reshape(9 * chans, 128) for j in range(2)], axis=1
        )

    def pair(step, carry):
        y2 = 2 * step
        cot_cells = two_rows(cot_pad, y2, 128)
        stacked = jnp.dot(wbt[...], cot_cells, preferred_element_type=F32)
        for j in range(2):
            back = combine(stacked[:, 128 * j : 128 * (j + 1)], 64) * 0.125
            high, low = split(back)
            wide = jnp.dot(high, spread, preferred_element_type=F32) + jnp.dot(
                low, spread, preferred_element_type=F32
            )
            grads, fields = [], []
            bias = jnp.zeros((64, 256), F32)
            for x in range(2):
                for i in range(2):
                    y = 2 * (y2 + j) + i
                    kept = mask[x, y].astype(F32)
                    grad = jnp.where(kept > 0, wide, 0.3 * wide).astype(BF16)
                    exact = grad.astype(F32)
                    bias = bias + exact
                    grads.append(
                        jnp.concatenate(
                            [shifted(exact, 1).astype(BF16), grad, shifted(exact, -1).astype(BF16)], axis=0
                        )
                    )
                    fields.append(vol_pad[pl.ds(x, 3), pl.ds(y, 3)].reshape(288, 256))
            gw1[:, :288] += lax.dot_general(
                jnp.concatenate(grads, axis=1),
                jnp.concatenate(fields, axis=1),
                (((1,), (1,)), ((), ())),
                preferred_element_type=F32,
            )
            gw1[64:128, 288:289] += jnp.sum(bias, axis=1, keepdims=True)
        pool_cells = two_rows(pool_pad, y2, 64)
        stacked = jnp.dot(wf[...], pool_cells, preferred_element_type=F32)
        own = []
        for j in range(2):
            second[y2 + j] = combine(stacked[:, 128 * j : 128 * (j + 1)], 128)
            cot = cot_pad[1, y2 + j + 1].astype(F32)
            gw2[128:256, 576:577] += jnp.sum(cot, axis=1, keepdims=True)
            own.append(
                jnp.concatenate([shifted(cot, 1), cot, shifted(cot, -1)], axis=0).astype(BF16)
            )
        gw2[:, :576] += lax.dot_general(
            jnp.concatenate(own, axis=1), pool_cells, (((1,), (1,)), ((), ())), preferred_element_type=F32
        )
        return carry

    lax.fori_loop(0, 4, pair, 0)


def reduce_kernel(
    scale, second, gw2, gw1, b2, second_out, w2_out, w1_out,
    send2, send1, recv2, recv1, part, parts, whole, all1, local_sem,
    os_, or_, s2, r2, s1, r1, ts, tr, gs, gr, us, ur,
):
    sx, sy, rep = place()
    group = sx * 2 + rep
    peers = [(sx, (sy + d) % 8, rep) for d in range(1, 8)]
    mates = []
    for e in range(1, 16):
        other = (group + e) % 16
        mates.append((other // 2, sy, other % 2))
    send2[...] = gw2[...].astype(BF16)
    for j in range(8):
        send1[j, 0:24] = gw1[24 * j : 24 * (j + 1)].astype(BF16)
        send1[j, 24:32] = jnp.zeros((8, 384), BF16)
    part[...] = jnp.zeros_like(part)
    greet(peers + mates)
    first = []
    for d in range(1, 8):
        j = (sy + d) % 8
        rows = pl.ds(pl.multiple_of(16 * j, 16), 16)
        first.append(remote(send2.at[:, rows, :], recv2.at[d], s2.at[d], r2.at[d], peers[d - 1]))
        first.append(remote(send1.at[j], recv1.at[d], s1.at[d], r1.at[d], peers[d - 1]))
    for copy in first:
        copy.start()
    here = pl.ds(pl.multiple_of(8 * sy, 8), 8)
    outs = []
    for d in range(1, 8):
        rows = pl.ds(pl.multiple_of(16 * ((sy + d) % 8), 16), 16)
        outs.append(remote(second.at[rows], second_out.at[:, here, :], os_.at[d], or_.at[d], peers[d - 1]))
    for copy in outs:
        copy.start()
    mine = pl.ds(pl.multiple_of(16 * sy, 16), 16)
    kept = pltpu.make_async_copy(second.at[mine], second_out.at[:, here, :], local_sem)
    kept.start()
    for copy in first:
        copy.wait()
    sum2 = gw2[:, mine, :]
    sum1 = gw1[pl.ds(pl.multiple_of(24 * sy, 8), 24), :]
    for d in range(1, 8):
        sum2 = sum2 + recv2[d].astype(F32)
        sum1 = sum1 + recv1[d, 0:24].astype(F32)
    for k in range(3):
        for h in range(2):
            for l in range(5):
                part[(k * 2 + h) * 5 + l] = sum2[k, 8 * h : 8 * h + 8, 128 * l : 128 * (l + 1)]
    for r in range(3):
        for l in range(3):
            part[30 + r * 3 + l] = sum1[8 * r : 8 * r + 8, 128 * l : 128 * (l + 1)]
    second_phase = []
    for e in range(1, 16):
        other = (group + e) % 16
        second_phase.append(
            remote(part.at[pl.ds(3 * other, 3)], parts.at[e], ts.at[e], tr.at[e], mates[e - 1])
        )
    for copy in second_phase:
        copy.start()
    kept.wait()
    for copy in outs:
        copy.wait()
    second_out[...] += b2[...]
    for copy in second_phase:
        copy.wait()
    own = pl.ds(3 * group, 3)
    total = part[own]
    for e in range(1, 16):
        total = total + parts[e]
    whole[own] = total * scale
    third = []
    for e in range(1, 16):
        third.append(remote(whole.at[own], whole.at[own], gs.at[e], gr.at[e], mates[e - 1]))
    for copy in third:
        copy.start()
    for copy in third:
        copy.wait()
    last = []
    for d in range(1, 8):
        last.append(remote(whole.at[pl.ds(30, 9)], all1.at[sy], us.at[d], ur.at[d], peers[d - 1]))
    for copy in last:
        copy.start()
    all1[sy] = whole[30:39]
    for k in range(3):
        for h in range(2):
            for l in range(5):
                w2_out[k, 8 * h : 8 * h + 8, 128 * l : 128 * (l + 1)] = whole[(k * 2 + h) * 5 + l]
    for copy in last:
        copy.wait()
    for j in range(8):
        for r in range(3):
            for l in range(3):
                w1_out[24 * j + 8 * r : 24 * j + 8 * r + 8, 128 * l : 128 * (l + 1)] = all1[j, r * 3 + l]


def call(body, outs, scratch=(), collective=None, count=1):
    params = dict(vmem_limit_bytes=LIMIT)
    if collective is not None:
        params.update(collective_id=collective, has_side_effects=True)
    return pl.pallas_call(
        body,
        out_shape=tuple(jax.ShapeDtypeStruct(s, t) for s, t in outs),
        in_specs=[VMEM] * count,
        out_specs=tuple([VMEM] * len(outs)),
        scratch_shapes=list(scratch),
        compiler_params=pltpu.CompilerParams(**params),
    )


def dma(n):
    return pltpu.SemaphoreType.DMA((n,))


def per_device(volume, first_kernel, first_bias, second_kernel, second_bias, cotangent):
    scale = 1.0 / math.sqrt(131072)
    vol = volume[0].transpose(1, 2, 0, 3)
    cot = jnp.pad(cotangent[0, :, 0].transpose(1, 0, 2), ((1, 1), (0, 0), (0, 0)))
    w1 = first_kernel.transpose(4, 0, 2, 3, 1).reshape(192, 288)
    wf = second_kernel.transpose(4, 0, 2, 3, 1).reshape(3, 16, 576)
    wb = second_kernel[:, :, ::-1, ::-1, ::-1].transpose(2, 3, 0, 4, 1).reshape(9, 16, 192)
    vol_pad, cot_pad, wf_all, wb_all = call(
        spread_kernel,
        [((4, 18, 32, 256), BF16), ((3, 10, 128, 128), BF16), ((3, 128, 576), BF16), ((9, 128, 192), BF16)],
        [dma(4), dma(8), dma(8), dma(8), dma(8), dma(16), dma(16), dma(16), dma(16)],
        0,
        4,
    )(vol, cot, wf, wb)
    pooled, mask = call(
        first_kernel_body, [((1, 8, 64, 128), BF16), ((2, 16, 64, 256), BF16)], count=3
    )(vol_pad, w1, first_bias[:, None])
    (pool_pad,) = call(
        halo_kernel, [((3, 10, 64, 128), BF16)], [pltpu.SemaphoreType.DMA, dma(8), dma(8)], 1
    )(pooled)
    wbt = wb_all.reshape(1152, 192).T
    second, gw2, gw1 = call(
        second_kernel_body, [((8, 128, 128), F32), ((384, 640), F32), ((192, 384), F32)], count=6
    )(vol_pad, cot_pad, wf_all.reshape(384, 576), wbt, pool_pad, mask)
    second_out, w2_sum, w1_sum = call(
        lambda *refs: reduce_kernel(scale, *refs),
        [((16, 64, 128), F32), ((3, 16, 640), F32), ((192, 384), F32)],
        [
            pltpu.VMEM((3, 128, 640), BF16),
            pltpu.VMEM((8, 32, 384), BF16),
            pltpu.VMEM((8, 3, 16, 640), BF16),
            pltpu.VMEM((8, 32, 384), BF16),
            pltpu.VMEM((48, 8, 128), F32),
            pltpu.VMEM((16, 3, 8, 128), F32),
            pltpu.VMEM((48, 8, 128), F32),
            pltpu.VMEM((8, 9, 8, 128), F32),
            pltpu.SemaphoreType.DMA,
        ]
        + [dma(8)] * 6
        + [dma(16)] * 4
        + [dma(8)] * 2,
        2,
        4,
    )(second.transpose(1, 0, 2), gw2.reshape(3, 128, 640), gw1, second_bias[:, None, None])
    gw2_out = w2_sum[:, :, :576].reshape(3, 16, 3, 3, 64).transpose(1, 4, 2, 3, 0)
    gw1_out = w1_sum[:, :288].reshape(3, 64, 3, 3, 32).transpose(1, 4, 2, 3, 0)
    return (
        second_out[None, :, None],
        gw1_out,
        w1_sum[64:128, 288],
        gw2_out,
        w2_sum[1, :, 576],
    )


def solution(mesh):
    placed = (
        P("rep", None, "sx", "sy", None),
        P(),
        P(),
        P("sy", None, None, None, None),
        P("sy"),
        P("rep", "sy", "sx", None, None),
    )
    return jax.shard_map(
        per_device,
        mesh=mesh,
        in_specs=placed,
        out_specs=(
            P("rep", "sy", "sx", None, None),
            P(),
            P(),
            P("sy", None, None, None, None),
            P("sy"),
        ),
        check_vma=False,
    )
```

```python
import math

import jax
import jax.numpy as jnp
from jax import lax
from jax.experimental import pallas as pl
from jax.experimental.pallas import tpu as pltpu
from jax.sharding import PartitionSpec as P

MESH = pl.DeviceIdType.MESH
BF16 = jnp.bfloat16
F32 = jnp.float32
NEIGHBOURS = [(dx, dy) for dx in (-1, 0, 1) for dy in (-1, 0, 1) if (dx, dy) != (0, 0)]
VMEM = pl.BlockSpec(memory_space=pltpu.VMEM)
LIMIT = 60 * 1024 * 1024


def place():
    return lax.axis_index("sx"), lax.axis_index("sy"), lax.axis_index("rep")


def remote(src, dst, send, recv, device):
    return pltpu.make_async_remote_copy(
        src_ref=src, dst_ref=dst, send_sem=send, recv_sem=recv, device_id=device, device_id_type=MESH
    )


def greet(devices):
    barrier = pltpu.get_barrier_semaphore()
    for device in devices:
        pl.semaphore_signal(barrier, inc=1, device_id=device, device_id_type=MESH)
    pl.semaphore_wait(barrier, len(devices))


def halo_copies(src, dst, send, recv):
    sx, sy, rep = place()
    cells_x, cells_y = src.shape[0], src.shape[1]
    rim_x, rim_y = cells_x + 1, cells_y + 1
    copies = []
    for k, (dx, dy) in enumerate(NEIGHBOURS):
        from_x = {1: pl.ds(cells_x - 1, 1), -1: pl.ds(0, 1), 0: pl.ds(0, cells_x)}[dx]
        from_y = {1: pl.ds(cells_y - 1, 1), -1: pl.ds(0, 1), 0: pl.ds(0, cells_y)}[dy]
        to_x = {1: pl.ds(0, 1), -1: pl.ds(rim_x, 1), 0: pl.ds(1, cells_x)}[dx]
        to_y = {1: pl.ds(0, 1), -1: pl.ds(rim_y, 1), 0: pl.ds(1, cells_y)}[dy]
        device = ((sx + (dx + 8)) % 8, (sy + (dy + 8)) % 8, rep)
        copies.append(remote(src.at[from_x, from_y], dst.at[to_x, to_y], send.at[k], recv.at[k], device))
    return copies


def clear_rim(dst):
    sx, sy, _ = place()
    rim_x, rim_y = dst.shape[0] - 1, dst.shape[1] - 1

    @pl.when(sx == 0)
    def _():
        dst[0] = jnp.zeros(dst.shape[1:], dst.dtype)

    @pl.when(sx == 7)
    def _():
        dst[rim_x] = jnp.zeros(dst.shape[1:], dst.dtype)

    @pl.when(sy == 0)
    def _():
        dst[:, 0] = jnp.zeros((dst.shape[0],) + dst.shape[2:], dst.dtype)

    @pl.when(sy == 7)
    def _():
        dst[:, rim_y] = jnp.zeros((dst.shape[0],) + dst.shape[2:], dst.dtype)


def shifted(block, step):
    width = block.shape[-1]
    lanes = lax.broadcasted_iota(jnp.int32, block.shape, block.ndim - 1)
    if step == 1:
        return jnp.where(lanes == width - 1, 0.0, pltpu.roll(block, width - 1, block.ndim - 1))
    return jnp.where(lanes == 0, 0.0, pltpu.roll(block, 1, block.ndim - 1))


def combine(stacked, chans):
    return (
        stacked[chans : 2 * chans] + shifted(stacked[:chans], -1) + shifted(stacked[2 * chans :], 1)
    )


def split(block):
    high = block.astype(BF16)
    return high, (block - high.astype(F32)).astype(BF16)


def pairs_of(shape, across):
    rows = lax.broadcasted_iota(jnp.int32, shape, 0)
    columns = lax.broadcasted_iota(jnp.int32, shape, 1)
    hit = (rows // 2 == columns) if across == 0 else (columns // 2 == rows)
    return jnp.where(hit, 1.0, 0.0).astype(BF16)


def first_rows(vol_pad, w1, bias, pooled, mask, start, stop):
    gather = pairs_of((256, 128), 0)

    def row(y2, carry):
        total = jnp.zeros((64, 256), F32)
        for x in range(2):
            for j in range(2):
                y = 2 * y2 + j
                cells = vol_pad[pl.ds(x, 3), pl.ds(y, 3)].reshape(288, 256)
                pre = combine(jnp.dot(w1[0:192, 0:288], cells, preferred_element_type=F32), 64) + bias
                mask[x, y] = jnp.where(pre > 0, 1.0, 0.0).astype(BF16)
                total = total + jnp.where(pre > 0, pre, 0.3 * pre)
        high, low = split(total)
        summed = jnp.dot(high, gather, preferred_element_type=F32) + jnp.dot(
            low, gather, preferred_element_type=F32
        )
        pooled[0, y2] = (summed * 0.125).astype(BF16)
        return carry

    lax.fori_loop(start, stop, row, 0)


def two_rows(ref, y, chans):
    return jnp.concatenate(
        [ref[:, pl.ds(y + j, 3)].reshape(9 * chans, 128) for j in range(2)], axis=1
    )


def across(a, b):
    return lax.dot_general(a, b, (((1,), (1,)), ((), ())), preferred_element_type=F32)


def back_rows(vol_pad, cot_pad, wbt, mask, gw1):
    spread = pairs_of((128, 256), 1)
    ones = jnp.ones((16, 1024), BF16)

    def pair(step, carry):
        y2 = 2 * step
        stacked = jnp.dot(wbt[...], two_rows(cot_pad, y2, 128), preferred_element_type=F32)
        for j in range(2):
            back = combine(stacked[:, 128 * j : 128 * (j + 1)], 64) * 0.125
            high, low = split(back)
            wide = jnp.dot(high, spread, preferred_element_type=F32) + jnp.dot(
                low, spread, preferred_element_type=F32
            )
            grads, fields = [], []
            for x in range(2):
                for i in range(2):
                    y = 2 * (y2 + j) + i
                    kept = mask[x, y].astype(F32)
                    grad = jnp.where(kept > 0, wide, 0.3 * wide)
                    grads.append(
                        jnp.concatenate([shifted(grad, 1), grad, shifted(grad, -1)], axis=0).astype(BF16)
                    )
                    fields.append(vol_pad[pl.ds(x, 3), pl.ds(y, 3)].reshape(288, 256))
            cells = jnp.concatenate([jnp.concatenate(fields, axis=1), ones], axis=0)
            gw1[0:304, 0:192] += across(cells, jnp.concatenate(grads, axis=1))
        return carry

    lax.fori_loop(0, 4, pair, 0)


def second_rows(cot_pad, wf_all, pool_pad, second):
    def pair(step, carry):
        y2 = 2 * step
        weights = wf_all[...].reshape(384, 640)[:, 0:576]
        stacked = jnp.dot(weights, two_rows(pool_pad, y2, 64), preferred_element_type=F32)
        for j in range(2):
            second[y2 + j] = combine(stacked[:, 128 * j : 128 * (j + 1)], 128).astype(BF16)
        return carry

    lax.fori_loop(0, 4, pair, 0)


def second_grads(cot_pad, pool_pad, gw2):
    ones = jnp.ones((16, 256), BF16)

    def pair(step, carry):
        y2 = 2 * step
        cells = jnp.concatenate([two_rows(pool_pad, y2, 64), ones], axis=0)
        own = []
        for j in range(2):
            cot = cot_pad[1, y2 + j + 1].astype(F32)
            own.append(
                jnp.concatenate([shifted(cot, 1), cot, shifted(cot, -1)], axis=0).astype(BF16)
            )
        gw2[:, 0:592] += across(jnp.concatenate(own, axis=1), cells)
        return carry

    lax.fori_loop(0, 4, pair, 0)


def whole_kernel(
    vol, cot, k1, b1, k2, rows_out, gw2_out, gb2_out, gw1_out, gb1_out,
    cot_src, wf_own, vol_pad, cot_pad, wf_all, w1t, w1, wbt, pooled, pool_pad, mask, second, gw1, gw2,
    send1, recv1, part1, parts1, whole1, all1, send2, recv2, part2, parts2, whole2,
    ls, vs, vr, cs, cr, fs, fr, ws, wr, xs, xr, ps, pr, os_, or_,
    s1, r1, t1, q1, g1, h1, u1, v1, s2, r2, t2, q2, g2, h2,
):
    sx, sy, rep = place()
    core = sx % 2
    left, right = (sx + 7) % 8, (sx + 1) % 8
    partner = (sx + 1 - 2 * core, sy, rep)
    group = sx * 2 + rep
    peers = [(sx, (sy + d) % 8, rep) for d in range(1, 8)]
    mates = []
    for e in range(1, 16):
        other = (group + e) % 16
        mates.append((other // 2, sy, other % 2))
    mine = pl.ds(pl.multiple_of(16 * sy, 16), 16)

    def theirs(d):
        return pl.ds(pl.multiple_of(16 * ((sy + d) % 8), 16), 16)

    cot_src[0] = jnp.zeros((16, 128), BF16)
    cot_src[65] = jnp.zeros((16, 128), BF16)
    cot_src[1:65] = cot[...]
    for k in range(9):
        for z in range(3):
            wf_own[z, :, 64 * k : 64 * k + 64] = k2[3 * k + z]
    wf_own[:, :, 576:640] = jnp.zeros((3, 16, 64), BF16)
    greet(
        [((sx + (dx + 8)) % 8, (sy + (dy + 8)) % 8, rep) for dx in (-1, 1) for dy in (-1, 1)]
        + peers
        + mates
    )
    halo = halo_copies(vol, vol_pad, vs, vr)
    for copy in halo:
        copy.start()
    exchange = []
    for d in range(1, 8):
        source = cot_src.at[pl.ds(8 * ((sy + d) % 8), 10)]
        exchange.append(remote(source, cot_pad.at[1, :, mine, :], cs.at[d], cr.at[d], peers[d - 1]))
    for copy in exchange:
        copy.start()
    planes = pl.ds(core, 2)
    weights = []
    for d in range(1, 8):
        weights.append(
            remote(wf_own.at[planes], wf_all.at[planes, mine, :], ws.at[d], wr.at[d], peers[d - 1])
        )
    for copy in weights:
        copy.start()
    own_cot = cot_src.at[pl.ds(8 * sy, 10)]
    locals_ = [
        pltpu.make_async_copy(vol, vol_pad.at[pl.ds(1, 2), pl.ds(1, 16)], ls.at[0]),
        pltpu.make_async_copy(own_cot, cot_pad.at[1, :, mine, :], ls.at[1]),
        pltpu.make_async_copy(wf_own, wf_all.at[:, mine, :], ls.at[2]),
    ]
    for copy in locals_:
        copy.start()
    forwards = []

    def forward(d):
        rows = theirs(8 - d)
        source = cot_pad.at[1, :, rows, :] if d else own_cot
        both = [
            remote(source, cot_pad.at[2, :, rows, :], fs.at[d], fr.at[d], (left, sy, rep)),
            remote(source, cot_pad.at[0, :, rows, :], fs.at[8 + d], fr.at[8 + d], (right, sy, rep)),
        ]
        for copy in both:
            copy.start()
        forwards.extend(both)

    forward(0)
    for k in range(9):
        for z in range(3):
            w1t[32 * k : 32 * k + 32, 64 * z : 64 * z + 64] = k1[3 * k + z]
    w1t[288:384, :] = jnp.zeros((96, 256), BF16)
    w1t[0:288, 192:256] = jnp.zeros((288, 64), BF16)
    w1[...] = w1t[...].T
    square = (64, 64)
    diagonal = lax.broadcasted_iota(jnp.int32, square, 0) == lax.broadcasted_iota(jnp.int32, square, 1)
    bias = jnp.sum(jnp.where(diagonal, b1[...], 0.0), axis=1, keepdims=True)
    gw1[...] = jnp.zeros_like(gw1)
    gw2[...] = jnp.zeros_like(gw2)
    part1[...] = jnp.zeros_like(part1)
    part2[...] = jnp.zeros_like(part2)
    for copy in locals_ + halo:
        copy.wait()
    clear_rim(vol_pad)
    first_rows(vol_pad, w1, bias, pooled, mask, 0, 4)
    for d in range(1, 8):
        exchange[d - 1].wait_recv()
        forward(d)
    first_rows(vol_pad, w1, bias, pooled, mask, 4, 8)
    pool_halo = halo_copies(pooled, pool_pad, ps, pr)
    for copy in pool_halo:
        copy.start()
    pool_pad[1, 1:9] = pooled[0]
    share = []
    plane = pl.ds(2 * core, 1)
    for d in range(1, 8):
        weights[d - 1].wait_recv()
        rows = theirs(8 - d)
        share.append(
            remote(wf_all.at[plane, rows, :], wf_all.at[plane, rows, :], xs.at[d], xr.at[d], partner)
        )
        share[-1].start()
    for copy in forwards + share:
        copy.wait()
    for copy in exchange + weights:
        copy.wait_send()

    @pl.when(sx == 0)
    def _():
        cot_pad[0] = jnp.zeros(cot_pad.shape[1:], BF16)

    @pl.when(sx == 7)
    def _():
        cot_pad[2] = jnp.zeros(cot_pad.shape[1:], BF16)

    for z in range(3):
        turned = wf_all[z].T
        for k in range(9):
            wbt[64 * (2 - z) : 64 * (3 - z), 128 * (8 - k) : 128 * (9 - k)] = turned[64 * k : 64 * k + 64]
    back_rows(vol_pad, cot_pad, wbt, mask, gw1)
    for j in range(8):
        send1[j] = gw1[40 * j : 40 * (j + 1)].astype(BF16)
    first1 = []
    for d in range(1, 8):
        first1.append(remote(send1.at[(sy + d) % 8], recv1.at[d], s1.at[d], r1.at[d], peers[d - 1]))
    for copy in first1:
        copy.start()
    for copy in pool_halo:
        copy.wait()
    clear_rim(pool_pad)
    second_rows(cot_pad, wf_all, pool_pad, second)
    here = pl.ds(pl.multiple_of(8 * sy, 8), 8)
    outs = []
    for d in range(1, 8):
        outs.append(remote(second.at[:, theirs(d), :], rows_out.at[here], os_.at[d], or_.at[d], peers[d - 1]))
    for copy in outs:
        copy.start()
    kept = pltpu.make_async_copy(second.at[:, mine, :], rows_out.at[here], ls.at[3])
    kept.start()
    second_grads(cot_pad, pool_pad, gw2)
    send2[...] = gw2[...].reshape(3, 128, 640).astype(BF16)
    first2 = []
    for d in range(1, 8):
        first2.append(remote(send2.at[:, theirs(d), :], recv2.at[d], s2.at[d], r2.at[d], peers[d - 1]))
    for copy in first2:
        copy.start()
    for copy in first1:
        copy.wait()
    sum1 = gw1[pl.ds(pl.multiple_of(40 * sy, 8), 40), :]
    for d in range(1, 8):
        sum1 = sum1 + recv1[d].astype(F32)
    for r in range(5):
        for l in range(2):
            part1[2 * r + l] = sum1[8 * r : 8 * r + 8, 128 * l : 128 * (l + 1)]
    reduce1 = []
    for e in range(1, 16):
        other = (group + e) % 16
        reduce1.append(remote(part1.at[other], parts1.at[e], t1.at[e], q1.at[e], mates[e - 1]))
    for copy in reduce1:
        copy.start()
    for copy in first2:
        copy.wait()
    sum2 = jnp.concatenate(
        [gw2[pl.ds(pl.multiple_of(128 * z + 16 * sy, 16), 16), :][None] for z in range(3)], axis=0
    )
    for d in range(1, 8):
        sum2 = sum2 + recv2[d].astype(F32)
    for z in range(3):
        for h in range(2):
            for l in range(5):
                part2[(z * 2 + h) * 5 + l] = sum2[z, 8 * h : 8 * h + 8, 128 * l : 128 * (l + 1)]
    reduce2 = []
    for e in range(1, 16):
        other = (group + e) % 16
        reduce2.append(remote(part2.at[pl.ds(2 * other, 2)], parts2.at[e], t2.at[e], q2.at[e], mates[e - 1]))
    for copy in reduce2:
        copy.start()
    for copy in reduce1:
        copy.wait()
    total1 = part1[group]
    for e in range(1, 16):
        total1 = total1 + parts1[e]
    whole1[group] = total1
    gather1 = []
    for e in range(1, 16):
        gather1.append(remote(whole1.at[group], whole1.at[group], g1.at[e], h1.at[e], mates[e - 1]))
    for copy in gather1:
        copy.start()
    for copy in reduce2:
        copy.wait()
    own = pl.ds(2 * group, 2)
    total2 = part2[own]
    for e in range(1, 16):
        total2 = total2 + parts2[e]
    whole2[own] = total2
    gather2 = []
    for e in range(1, 16):
        gather2.append(remote(whole2.at[own], whole2.at[own], g2.at[e], h2.at[e], mates[e - 1]))
    for copy in gather2:
        copy.start()
    for copy in gather1:
        copy.wait()
    last1 = []
    for d in range(1, 8):
        last1.append(remote(whole1.at[pl.ds(0, 10)], all1.at[sy], u1.at[d], v1.at[d], peers[d - 1]))
    for copy in last1:
        copy.start()
    all1[sy] = whole1[0:10]
    for copy in gather2:
        copy.wait()
    for z in range(3):
        for h in range(2):
            for l in range(5):
                tile = whole2[(z * 2 + h) * 5 + l]
                gw2_out[2 * l * 3 + z, 8 * h : 8 * h + 8, :] = tile[:, 0:64]
                if l < 4:
                    gw2_out[(2 * l + 1) * 3 + z, 8 * h : 8 * h + 8, :] = tile[:, 64:128]
    column = jnp.concatenate([whole2[14][:, 64:65], whole2[19][:, 64:65]], axis=0)
    square = (16, 16)
    diagonal = lax.broadcasted_iota(jnp.int32, square, 0) == lax.broadcasted_iota(jnp.int32, square, 1)
    gb2_out[...] = jnp.sum(jnp.where(diagonal, column, 0.0), axis=0, keepdims=True)
    kept.wait()
    for copy in outs:
        copy.wait()
    for copy in last1:
        copy.wait()
    for j in range(8):
        for r in range(5):
            at = 40 * j + 8 * r
            if at < 288:
                for z in range(3):
                    tile = all1[j, 2 * r + z // 2]
                    gw1_out[3 * (at // 32) + z, at % 32 : at % 32 + 8, :] = tile[
                        :, 64 * (z % 2) : 64 * (z % 2) + 64
                    ]
    gb1_out[...] = all1[7, 2][0:1, 64:128]


def dma(n):
    return pltpu.SemaphoreType.DMA((n,))


def per_device(volume, first_kernel, first_bias, second_kernel, second_bias, cotangent):
    scale = 1.0 / math.sqrt(131072)
    vol = volume[0].transpose(1, 2, 0, 3)
    cot = cotangent[0, :, 0].transpose(1, 0, 2)
    k1 = first_kernel.transpose(2, 3, 4, 1, 0).reshape(27, 32, 64)
    k2 = second_kernel.transpose(2, 3, 4, 0, 1).reshape(27, 16, 64)
    outs = [
        ((64, 16, 128), BF16), ((27, 16, 64), F32), ((1, 16), F32), ((27, 32, 64), F32), ((1, 64), F32)
    ]
    scratch = [
        ((66, 16, 128), BF16),
        ((3, 16, 640), BF16),
        ((4, 18, 32, 256), BF16),
        ((3, 10, 128, 128), BF16),
        ((3, 128, 640), BF16),
        ((384, 256), BF16),
        ((256, 384), BF16),
        ((192, 1152), BF16),
        ((1, 8, 64, 128), BF16),
        ((3, 10, 64, 128), BF16),
        ((2, 16, 64, 256), BF16),
        ((8, 128, 128), BF16),
        ((320, 256), F32),
        ((384, 640), F32),
        ((8, 40, 256), BF16),
        ((8, 40, 256), BF16),
        ((16, 8, 128), F32),
        ((16, 8, 128), F32),
        ((16, 8, 128), F32),
        ((8, 10, 8, 128), F32),
        ((3, 128, 640), BF16),
        ((8, 3, 16, 640), BF16),
        ((32, 8, 128), F32),
        ((16, 2, 8, 128), F32),
        ((32, 8, 128), F32),
    ]
    sems = [4, 8, 8, 8, 8, 16, 16, 8, 8, 8, 8, 8, 8, 8, 8, 8, 8, 16, 16, 16, 16, 8, 8, 8, 8, 16, 16, 16, 16]
    rows_out, gw2, gb2, gw1, gb1 = pl.pallas_call(
        whole_kernel,
        out_shape=tuple(jax.ShapeDtypeStruct(s, t) for s, t in outs),
        in_specs=[VMEM] * 5,
        out_specs=tuple([VMEM] * 5),
        scratch_shapes=[pltpu.VMEM(s, t) for s, t in scratch] + [dma(n) for n in sems],
        compiler_params=pltpu.CompilerParams(
            vmem_limit_bytes=LIMIT, collective_id=0, has_side_effects=True
        ),
    )(vol, cot, k1, first_bias[None], k2)
    second_out = rows_out.transpose(1, 0, 2).astype(F32) + second_bias[:, None, None]
    return (
        second_out[None, :, None],
        (scale * gw1).reshape(3, 3, 3, 32, 64).transpose(4, 3, 0, 1, 2),
        scale * gb1[0],
        (scale * gw2).reshape(3, 3, 3, 16, 64).transpose(3, 4, 0, 1, 2),
        scale * gb2[0],
    )


def solution(mesh):
    placed = (
        P("rep", None, "sx", "sy", None),
        P(),
        P(),
        P("sy", None, None, None, None),
        P("sy"),
        P("rep", "sy", "sx", None, None),
    )
    return jax.shard_map(
        per_device,
        mesh=mesh,
        in_specs=placed,
        out_specs=(
            P("rep", "sy", "sx", None, None),
            P(),
            P(),
            P("sy", None, None, None, None),
            P("sy"),
        ),
        check_vma=False,
    )
```

```python
import functools
import math

import jax
import jax.numpy as jnp
from jax import lax
from jax.experimental import pallas as pl
from jax.experimental.pallas import tpu as pltpu
from jax.sharding import PartitionSpec as P

MESH = pl.DeviceIdType.MESH
BF16 = jnp.bfloat16
F32 = jnp.float32
NEIGHBOURS = [(dx, dy) for dx in (-1, 0, 1) for dy in (-1, 0, 1) if (dx, dy) != (0, 0)]
VMEM = pl.BlockSpec(memory_space=pltpu.VMEM)
LIMIT = 60 * 1024 * 1024


def place():
    return lax.axis_index("sx"), lax.axis_index("sy"), lax.axis_index("rep")


def remote(src, dst, send, recv, device):
    return pltpu.make_async_remote_copy(
        src_ref=src, dst_ref=dst, send_sem=send, recv_sem=recv, device_id=device, device_id_type=MESH
    )


def halo_copies(src, dst, send, recv):
    sx, sy, rep = place()
    cells_x, cells_y = src.shape[0], src.shape[1]
    rim_x, rim_y = cells_x + 1, cells_y + 1
    copies = []
    for k, (dx, dy) in enumerate(NEIGHBOURS):
        from_x = {1: pl.ds(cells_x - 1, 1), -1: pl.ds(0, 1), 0: pl.ds(0, cells_x)}[dx]
        from_y = {1: pl.ds(cells_y - 1, 1), -1: pl.ds(0, 1), 0: pl.ds(0, cells_y)}[dy]
        to_x = {1: pl.ds(0, 1), -1: pl.ds(rim_x, 1), 0: pl.ds(1, cells_x)}[dx]
        to_y = {1: pl.ds(0, 1), -1: pl.ds(rim_y, 1), 0: pl.ds(1, cells_y)}[dy]
        device = ((sx + (dx + 8)) % 8, (sy + (dy + 8)) % 8, rep)
        copies.append(remote(src.at[from_x, from_y], dst.at[to_x, to_y], send.at[k], recv.at[k], device))
    return copies


def clear_rim(dst):
    sx, sy, _ = place()
    rim_x, rim_y = dst.shape[0] - 1, dst.shape[1] - 1

    @pl.when(sx == 0)
    def _():
        dst[0] = jnp.zeros(dst.shape[1:], dst.dtype)

    @pl.when(sx == 7)
    def _():
        dst[rim_x] = jnp.zeros(dst.shape[1:], dst.dtype)

    @pl.when(sy == 0)
    def _():
        dst[:, 0] = jnp.zeros((dst.shape[0],) + dst.shape[2:], dst.dtype)

    @pl.when(sy == 7)
    def _():
        dst[:, rim_y] = jnp.zeros((dst.shape[0],) + dst.shape[2:], dst.dtype)


def shifted(block, step):
    width = block.shape[-1]
    lanes = lax.broadcasted_iota(jnp.int32, block.shape, block.ndim - 1)
    if step == 1:
        return jnp.where(lanes == width - 1, 0.0, pltpu.roll(block, width - 1, block.ndim - 1))
    return jnp.where(lanes == 0, 0.0, pltpu.roll(block, 1, block.ndim - 1))


def combine(stacked, chans):
    return (
        stacked[chans : 2 * chans] + shifted(stacked[:chans], -1) + shifted(stacked[2 * chans :], 1)
    )


def split(block):
    high = block.astype(BF16)
    return high, (block - high.astype(F32)).astype(BF16)


def pairs_of(shape, across):
    rows = lax.broadcasted_iota(jnp.int32, shape, 0)
    columns = lax.broadcasted_iota(jnp.int32, shape, 1)
    hit = (rows // 2 == columns) if across == 0 else (columns // 2 == rows)
    return jnp.where(hit, 1.0, 0.0).astype(BF16)


def first_rows(vol_pad, w1, bias, pooled, mask, start, stop):
    gather = pairs_of((256, 128), 0)

    def row(y2, carry):
        total = jnp.zeros((64, 256), F32)
        for x in range(2):
            for j in range(2):
                y = 2 * y2 + j
                cells = vol_pad[pl.ds(x, 3), pl.ds(y, 3)].reshape(288, 256)
                pre = combine(jnp.dot(w1[0:192, 0:288], cells, preferred_element_type=F32), 64) + bias
                mask[x, y] = jnp.where(pre > 0, 1.0, 0.0).astype(BF16)
                total = total + jnp.where(pre > 0, pre, 0.3 * pre)
        high, low = split(total)
        summed = jnp.dot(high, gather, preferred_element_type=F32) + jnp.dot(
            low, gather, preferred_element_type=F32
        )
        pooled[0, y2] = (summed * 0.125).astype(BF16)
        return carry

    lax.fori_loop(start, stop, row, 0)


def two_rows(ref, y, chans):
    return jnp.concatenate(
        [ref[:, pl.ds(y + j, 3)].reshape(9 * chans, 128) for j in range(2)], axis=1
    )


def across(a, b):
    return lax.dot_general(a, b, (((1,), (1,)), ((), ())), preferred_element_type=F32)


def back_rows(vol_pad, cot_pad, wbt, mask, gw1):
    spread = pairs_of((128, 256), 1)
    ones = jnp.ones((16, 1024), BF16)

    def pair(step, carry):
        y2 = 2 * step
        stacked = jnp.dot(wbt[...], two_rows(cot_pad, y2, 128), preferred_element_type=F32)
        for j in range(2):
            back = combine(stacked[:, 128 * j : 128 * (j + 1)], 64) * 0.125
            high, low = split(back)
            wide = jnp.dot(high, spread, preferred_element_type=F32) + jnp.dot(
                low, spread, preferred_element_type=F32
            )
            grads, fields = [], []
            for x in range(2):
                for i in range(2):
                    y = 2 * (y2 + j) + i
                    kept = mask[x, y].astype(F32)
                    grad = jnp.where(kept > 0, wide, 0.3 * wide)
                    grads.append(
                        jnp.concatenate([shifted(grad, 1), grad, shifted(grad, -1)], axis=0).astype(BF16)
                    )
                    fields.append(vol_pad[pl.ds(x, 3), pl.ds(y, 3)].reshape(288, 256))
            cells = jnp.concatenate([jnp.concatenate(fields, axis=1), ones], axis=0)
            gw1[0:304, 0:192] += across(cells, jnp.concatenate(grads, axis=1))
        return carry

    lax.fori_loop(0, 4, pair, 0)


def second_rows(cot_pad, wf_all, pool_pad, second):
    def pair(step, carry):
        y2 = 2 * step
        weights = wf_all[...].reshape(384, 640)[:, 0:576]
        stacked = jnp.dot(weights, two_rows(pool_pad, y2, 64), preferred_element_type=F32)
        for j in range(2):
            second[y2 + j] = combine(stacked[:, 128 * j : 128 * (j + 1)], 128).astype(BF16)
        return carry

    lax.fori_loop(0, 4, pair, 0)


def second_grads(cot_pad, pooled, gw2):
    ones = jnp.ones((16, 256), BF16)

    def pair(step, carry):
        y2 = 2 * step
        own = []
        for j in range(2):
            cells = pooled[0, y2 + j].astype(F32)
            own.append(jnp.concatenate([shifted(cells, -1), cells, shifted(cells, 1)], axis=0).astype(BF16))
        fields = jnp.concatenate([jnp.concatenate(own, axis=1), ones], axis=0)
        gw2[:, 0:208] += across(two_rows(cot_pad, y2, 128), fields)
        return carry

    lax.fori_loop(0, 4, pair, 0)


def whole_kernel(
    vol, cot, k1, b1, k2, rows_out, whole2, all1,
    vol_src, cot_src, wf_own, vol_pad, cot_pad, wf_all, w1t, w1, wbt, pooled, pool_pad, mask, second, gw1, gw2,
    pack1, send1, recv1, part1, parts1, whole1, pack2, send2, recv2, part2, parts2,
    ls, vs, vr, cs, cr, fs, fr, ws, wr, xs, xr, ps, pr, os_, or_,
    s1, r1, t1, q1, g1, h1, u1, v1, s2, r2, t2, q2, g2, h2,
):
    sx, sy, rep = place()
    core = sx % 2
    left, right = (sx + 7) % 8, (sx + 1) % 8
    partner = (sx + 1 - 2 * core, sy, rep)
    peers = [(sx, (sy + d) % 8, rep) for d in range(1, 8)]
    column = [((sx + d) % 8, sy, rep) for d in range(1, 8)]
    group1, group2 = sy * 2 + rep, sx * 2 + rep
    mates1, mates2 = [], []
    for e in range(1, 16):
        other = (group1 + e) % 16
        mates1.append((sx, other // 2, other % 2))
        other = (group2 + e) % 16
        mates2.append((other // 2, sy, other % 2))
    mine = pl.ds(pl.multiple_of(16 * sy, 16), 16)

    def theirs(d):
        return pl.ds(pl.multiple_of(16 * ((sy + d) % 8), 16), 16)

    barrier = pltpu.get_barrier_semaphore()
    around = [((sx + (dx + 8)) % 8, (sy + (dy + 8)) % 8, rep) for dx in (-1, 1) for dy in (-1, 1)]
    opposite = [(sx, (sy + d) % 8, 1 - rep) for d in range(1, 8)]
    greeted = around + peers + opposite + mates2
    for device in greeted:
        pl.semaphore_signal(barrier, inc=1, device_id=device, device_id_type=MESH)
    vol_src[...] = jnp.stack([jnp.swapaxes(vol[:, x], 0, 1) for x in range(2)])
    cot_src[0] = jnp.zeros((16, 128), BF16)
    cot_src[65] = jnp.zeros((16, 128), BF16)
    cot_src[1:65] = jnp.swapaxes(cot[...], 0, 1)
    for k in range(9):
        for z in range(3):
            wf_own[z, :, 64 * k : 64 * k + 64] = k2[3 * k + z]
    wf_own[:, :, 576:640] = jnp.zeros((3, 16, 64), BF16)
    pl.semaphore_wait(barrier, len(greeted))
    halo = halo_copies(vol_src, vol_pad, vs, vr)
    for copy in halo:
        copy.start()
    order = (4, 1, 7, 3, 5, 2, 6)
    exchange = {}
    for d in order:
        source = cot_src.at[pl.ds(8 * ((sy + d) % 8), 10)]
        exchange[d] = remote(source, cot_pad.at[1, :, mine, :], cs.at[d], cr.at[d], peers[d - 1])
        exchange[d].start()
    planes = pl.ds(core, 2)
    weights = {}
    for d in order:
        weights[d] = remote(wf_own.at[planes], wf_all.at[planes, mine, :], ws.at[d], wr.at[d], peers[d - 1])
        weights[d].start()
    own_cot = cot_src.at[pl.ds(8 * sy, 10)]
    locals_ = [
        pltpu.make_async_copy(vol_src, vol_pad.at[pl.ds(1, 2), pl.ds(1, 16)], ls.at[0]),
        pltpu.make_async_copy(own_cot, cot_pad.at[1, :, mine, :], ls.at[1]),
        pltpu.make_async_copy(wf_own, wf_all.at[:, mine, :], ls.at[2]),
    ]
    for copy in locals_:
        copy.start()
    forwards = []

    def forward(d):
        rows = theirs(8 - d)
        source = cot_pad.at[1, :, rows, :] if d else own_cot
        both = [
            remote(source, cot_pad.at[2, :, rows, :], fs.at[d], fr.at[d], (left, sy, rep)),
            remote(source, cot_pad.at[0, :, rows, :], fs.at[8 + d], fr.at[8 + d], (right, sy, rep)),
        ]
        for copy in both:
            copy.start()
        forwards.extend(both)

    forward(0)
    for k in range(9):
        for z in range(3):
            w1t[32 * k : 32 * k + 32, 64 * z : 64 * z + 64] = k1[3 * k + z]
    w1t[288:384, :] = jnp.zeros((96, 256), BF16)
    w1t[0:288, 192:256] = jnp.zeros((288, 64), BF16)
    w1[...] = w1t[...].T
    square = (64, 64)
    diagonal = lax.broadcasted_iota(jnp.int32, square, 0) == lax.broadcasted_iota(jnp.int32, square, 1)
    bias = jnp.sum(jnp.where(diagonal, b1[...], 0.0), axis=1, keepdims=True)
    gw1[...] = jnp.zeros_like(gw1)
    gw2[...] = jnp.zeros_like(gw2)
    pack1[28:32] = jnp.zeros((4, 16, 128), F32)
    part1[8:16] = jnp.zeros((8, 8, 128), F32)
    part2[28:32] = jnp.zeros((4, 8, 128), F32)
    for copy in locals_ + halo:
        copy.wait()
    clear_rim(vol_pad)
    first_rows(vol_pad, w1, bias, pooled, mask, 0, 1)
    for d in order[:5]:
        exchange[d].wait_recv()
        forward(d)
    first_rows(vol_pad, w1, bias, pooled, mask, 1, 2)
    for d in order[5:]:
        exchange[d].wait_recv()
        forward(d)
    first_rows(vol_pad, w1, bias, pooled, mask, 2, 5)
    share = []
    plane = pl.ds(2 * core, 1)
    for d in order:
        weights[d].wait_recv()
        rows = theirs(8 - d)
        share.append(
            remote(wf_all.at[plane, rows, :], wf_all.at[plane, rows, :], xs.at[d], xr.at[d], partner)
        )
        share[-1].start()
    first_rows(vol_pad, w1, bias, pooled, mask, 5, 8)
    pool_halo = halo_copies(pooled, pool_pad, ps, pr)
    for copy in pool_halo:
        copy.start()
    pool_pad[1, 1:9] = pooled[0]
    for copy in forwards:
        copy.wait()

    @pl.when(sx == 0)
    def _():
        cot_pad[0] = jnp.zeros(cot_pad.shape[1:], BF16)

    @pl.when(sx == 7)
    def _():
        cot_pad[2] = jnp.zeros(cot_pad.shape[1:], BF16)

    second_grads(cot_pad, pooled, gw2)
    for i in range(9):
        pack2[i] = gw2[128 * i : 128 * (i + 1), 0:128]
    for i in range(5):
        last = gw2[512:640, 192:256] if i == 4 else gw2[128 * (2 * i + 1) : 128 * (2 * i + 2), 128:192]
        pack2[9 + i] = jnp.concatenate([gw2[256 * i : 256 * i + 128, 128:192], last], axis=1)
    send2[...] = pack2[...].astype(BF16)
    first2 = []
    for d in order:
        first2.append(remote(send2.at[:, theirs(d), :], recv2.at[d], s2.at[d], r2.at[d], peers[d - 1]))
    for copy in first2:
        copy.start()
    for copy in share:
        copy.wait()
    for d in order:
        exchange[d].wait_send()
        weights[d].wait_send()
    for z in range(3):
        turned = wf_all[z].T
        for k in range(9):
            wbt[64 * (2 - z) : 64 * (3 - z), 128 * (8 - k) : 128 * (9 - k)] = turned[64 * k : 64 * k + 64]
    back_rows(vol_pad, cot_pad, wbt, mask, gw1)
    for i in range(18):
        pack1[i] = gw1[16 * i : 16 * (i + 1), 0:128]
    for i in range(9):
        pack1[18 + i] = jnp.concatenate(
            [gw1[16 * i : 16 * (i + 1), 128:192], gw1[144 + 16 * i : 160 + 16 * i, 128:192]], axis=1
        )
    pack1[27] = gw1[288:304, 0:128]
    send1[...] = pack1[...].astype(BF16)
    first1 = []
    for d in range(1, 8):
        rows = pl.ds(4 * ((sx + d) % 8), 4)
        first1.append(remote(send1.at[rows], recv1.at[d], s1.at[d], r1.at[d], column[d - 1]))
    for copy in first1:
        copy.start()
    for copy in pool_halo:
        copy.wait()
    clear_rim(pool_pad)
    second_rows(cot_pad, wf_all, pool_pad, second)
    for copy in first1:
        copy.wait()
    sum1 = pack1[pl.ds(4 * sx, 4)]
    for d in range(1, 8):
        sum1 = sum1 + recv1[d].astype(F32)
    for i in range(4):
        for h in range(2):
            part1[2 * i + h] = sum1[i, 8 * h : 8 * h + 8]
    reduce1 = []
    for e in range(1, 16):
        other = (group1 + e) % 16
        reduce1.append(remote(part1.at[other], parts1.at[e], t1.at[e], q1.at[e], mates1[e - 1]))
    for copy in reduce1:
        copy.start()
    for copy in first2:
        copy.wait()
    sum2 = pack2[:, mine, :]
    for d in range(1, 8):
        sum2 = sum2 + recv2[d].astype(F32)
    for i in range(14):
        for h in range(2):
            part2[2 * i + h] = sum2[i, 8 * h : 8 * h + 8]
    reduce2 = []
    for e in range(1, 16):
        other = (group2 + e) % 16
        reduce2.append(remote(part2.at[pl.ds(2 * other, 2)], parts2.at[e], t2.at[e], q2.at[e], mates2[e - 1]))
    for copy in reduce2:
        copy.start()
    here = pl.ds(pl.multiple_of(8 * sy, 8), 8)
    outs = []
    for d in order:
        outs.append(remote(second.at[:, theirs(d), :], rows_out.at[here], os_.at[d], or_.at[d], peers[d - 1]))
    for copy in outs:
        copy.start()
    kept = pltpu.make_async_copy(second.at[:, mine, :], rows_out.at[here], ls.at[3])
    kept.start()
    for copy in reduce1:
        copy.wait()
    total1 = part1[group1]
    for e in range(1, 16):
        total1 = total1 + parts1[e]
    whole1[group1] = total1
    gather1 = []
    for e in range(1, 16):
        gather1.append(remote(whole1.at[group1], whole1.at[group1], g1.at[e], h1.at[e], mates1[e - 1]))
    for copy in gather1:
        copy.start()
    for copy in reduce2:
        copy.wait()
    own = pl.ds(2 * group2, 2)
    total2 = part2[own]
    for e in range(1, 16):
        total2 = total2 + parts2[e]
    whole2[own] = total2
    gather2 = []
    for e in range(1, 16):
        gather2.append(remote(whole2.at[own], whole2.at[own], g2.at[e], h2.at[e], mates2[e - 1]))
    for copy in gather2:
        copy.start()
    for copy in gather1:
        copy.wait()
    last1 = []
    for d in range(1, 8):
        last1.append(remote(whole1.at[pl.ds(0, 8)], all1.at[sx], u1.at[d], v1.at[d], column[d - 1]))
    for copy in last1:
        copy.start()
    all1[sx] = whole1[0:8]
    kept.wait()
    for copy in outs + gather2 + last1:
        copy.wait()


def final_kernel(scale, rows, whole2, all1, b2, second_out, gw2_out, gb2_out, gw1_out, gb1_out):
    square = (16, 16)
    diagonal = lax.broadcasted_iota(jnp.int32, square, 0) == lax.broadcasted_iota(jnp.int32, square, 1)
    bias = jnp.sum(jnp.where(diagonal, b2[...], 0.0), axis=1, keepdims=True)
    second_out[...] = jnp.swapaxes(rows[...].astype(F32) + bias[None], 0, 1)
    for h in range(2):
        at = slice(8 * h, 8 * h + 8)
        for i in range(9):
            tile = whole2[2 * i + h] * scale
            gw2_out[3 * (8 - i), at, :] = tile[:, 0:64]
            gw2_out[3 * (8 - i) + 1, at, :] = tile[:, 64:128]
        for i in range(5):
            tile = whole2[2 * (9 + i) + h] * scale
            gw2_out[3 * (8 - 2 * i) + 2, at, :] = tile[:, 0:64]
            if i < 4:
                gw2_out[3 * (7 - 2 * i) + 2, at, :] = tile[:, 64:128]
    column = jnp.concatenate([whole2[26][:, 64:65], whole2[27][:, 64:65]], axis=0) * scale
    gb2_out[...] = jnp.sum(jnp.where(diagonal, column, 0.0), axis=0, keepdims=True)
    for i in range(27):
        for h in range(2):
            tile = all1[i // 4, 2 * (i % 4) + h] * scale
            if i < 18:
                at = 16 * i + 8 * h
                for z in range(2):
                    gw1_out[3 * (at // 32) + z, at % 32 : at % 32 + 8, :] = tile[:, 64 * z : 64 * z + 64]
            else:
                for z in range(2):
                    at = 144 * z + 16 * (i - 18) + 8 * h
                    gw1_out[3 * (at // 32) + 2, at % 32 : at % 32 + 8, :] = tile[:, 64 * z : 64 * z + 64]
    gb1_out[...] = all1[6, 6][0:1, 64:128] * scale


def dma(n):
    return pltpu.SemaphoreType.DMA((n,))


def per_device(volume, first_kernel, first_bias, second_kernel, second_bias, cotangent):
    scale = 1.0 / math.sqrt(131072)
    k1 = first_kernel.transpose(2, 3, 4, 1, 0).reshape(27, 32, 64)
    k2 = second_kernel.transpose(2, 3, 4, 0, 1).reshape(27, 16, 64)
    outs = [((64, 16, 128), BF16), ((32, 8, 128), F32), ((8, 8, 8, 128), F32)]
    scratch = [
        ((2, 16, 32, 256), BF16),
        ((66, 16, 128), BF16),
        ((3, 16, 640), BF16),
        ((4, 18, 32, 256), BF16),
        ((3, 10, 128, 128), BF16),
        ((3, 128, 640), BF16),
        ((384, 256), BF16),
        ((256, 384), BF16),
        ((192, 1152), BF16),
        ((1, 8, 64, 128), BF16),
        ((3, 10, 64, 128), BF16),
        ((2, 16, 64, 256), BF16),
        ((8, 128, 128), BF16),
        ((304, 256), F32),
        ((1152, 256), F32),
        ((32, 16, 128), F32),
        ((32, 16, 128), BF16),
        ((8, 4, 16, 128), BF16),
        ((16, 8, 128), F32),
        ((16, 8, 128), F32),
        ((16, 8, 128), F32),
        ((14, 128, 128), F32),
        ((14, 128, 128), BF16),
        ((8, 14, 16, 128), BF16),
        ((32, 8, 128), F32),
        ((16, 2, 8, 128), F32),
    ]
    sems = [4, 8, 8, 8, 8, 16, 16, 8, 8, 8, 8, 8, 8, 8, 8, 8, 8, 16, 16, 16, 16, 8, 8, 8, 8, 16, 16, 16, 16]
    rows, whole2, all1 = pl.pallas_call(
        whole_kernel,
        out_shape=tuple(jax.ShapeDtypeStruct(s, t) for s, t in outs),
        in_specs=[VMEM] * 5,
        out_specs=tuple([VMEM] * 3),
        scratch_shapes=[pltpu.VMEM(s, t) for s, t in scratch] + [dma(n) for n in sems],
        compiler_params=pltpu.CompilerParams(
            vmem_limit_bytes=LIMIT, collective_id=0, has_side_effects=True
        ),
    )(volume[0], cotangent[0, :, 0], k1, first_bias[None], k2)
    finals = [((16, 64, 128), F32), ((27, 16, 64), F32), ((1, 16), F32), ((27, 32, 64), F32), ((1, 64), F32)]
    second_out, gw2, gb2, gw1, gb1 = pl.pallas_call(
        functools.partial(final_kernel, scale),
        out_shape=tuple(jax.ShapeDtypeStruct(s, t) for s, t in finals),
        in_specs=[VMEM] * 4,
        out_specs=tuple([VMEM] * 5),
        compiler_params=pltpu.CompilerParams(vmem_limit_bytes=LIMIT),
    )(rows, whole2, all1, second_bias[None])
    return (
        second_out[None, :, None],
        gw1.reshape(3, 3, 3, 32, 64).transpose(4, 3, 0, 1, 2),
        gb1[0],
        gw2.reshape(3, 3, 3, 16, 64).transpose(3, 4, 0, 1, 2),
        gb2[0],
    )


def solution(mesh):
    placed = (
        P("rep", None, "sx", "sy", None),
        P(),
        P(),
        P("sy", None, None, None, None),
        P("sy"),
        P("rep", "sy", "sx", None, None),
    )
    return jax.shard_map(
        per_device,
        mesh=mesh,
        in_specs=placed,
        out_specs=(
            P("rep", "sy", "sx", None, None),
            P(),
            P(),
            P("sy", None, None, None, None),
            P("sy"),
        ),
        check_vma=False,
    )
```

```python
import functools
import math

import jax
import jax.numpy as jnp
from jax import lax
from jax.experimental import pallas as pl
from jax.experimental.pallas import tpu as pltpu
from jax.sharding import PartitionSpec as P

MESH = pl.DeviceIdType.MESH
BF16 = jnp.bfloat16
F32 = jnp.float32
NEIGHBOURS = [(dx, dy) for dx in (-1, 0, 1) for dy in (-1, 0, 1) if (dx, dy) != (0, 0)]
VMEM = pl.BlockSpec(memory_space=pltpu.VMEM)
LIMIT = 60 * 1024 * 1024


def place():
    return lax.axis_index("sx"), lax.axis_index("sy"), lax.axis_index("rep")


def remote(src, dst, send, recv, device):
    return pltpu.make_async_remote_copy(
        src_ref=src, dst_ref=dst, send_sem=send, recv_sem=recv, device_id=device, device_id_type=MESH
    )


def halo_copies(src, dst, send, recv):
    sx, sy, rep = place()
    cells_x, cells_y = src.shape[0], src.shape[1]
    rim_x, rim_y = cells_x + 1, cells_y + 1
    copies = []
    for k, (dx, dy) in enumerate(NEIGHBOURS):
        from_x = {1: pl.ds(cells_x - 1, 1), -1: pl.ds(0, 1), 0: pl.ds(0, cells_x)}[dx]
        from_y = {1: pl.ds(cells_y - 1, 1), -1: pl.ds(0, 1), 0: pl.ds(0, cells_y)}[dy]
        to_x = {1: pl.ds(0, 1), -1: pl.ds(rim_x, 1), 0: pl.ds(1, cells_x)}[dx]
        to_y = {1: pl.ds(0, 1), -1: pl.ds(rim_y, 1), 0: pl.ds(1, cells_y)}[dy]
        device = ((sx + (dx + 8)) % 8, (sy + (dy + 8)) % 8, rep)
        copies.append(remote(src.at[from_x, from_y], dst.at[to_x, to_y], send.at[k], recv.at[k], device))
    return copies


def clear_rim(dst):
    sx, sy, _ = place()
    rim_x, rim_y = dst.shape[0] - 1, dst.shape[1] - 1

    @pl.when(sx == 0)
    def _():
        dst[0] = jnp.zeros(dst.shape[1:], dst.dtype)

    @pl.when(sx == 7)
    def _():
        dst[rim_x] = jnp.zeros(dst.shape[1:], dst.dtype)

    @pl.when(sy == 0)
    def _():
        dst[:, 0] = jnp.zeros((dst.shape[0],) + dst.shape[2:], dst.dtype)

    @pl.when(sy == 7)
    def _():
        dst[:, rim_y] = jnp.zeros((dst.shape[0],) + dst.shape[2:], dst.dtype)


def shifted(block, step):
    width = block.shape[-1]
    lanes = lax.broadcasted_iota(jnp.int32, block.shape, block.ndim - 1)
    if step == 1:
        return jnp.where(lanes == width - 1, 0.0, pltpu.roll(block, width - 1, block.ndim - 1))
    return jnp.where(lanes == 0, 0.0, pltpu.roll(block, 1, block.ndim - 1))


def combine(stacked, chans):
    return (
        stacked[chans : 2 * chans] + shifted(stacked[:chans], -1) + shifted(stacked[2 * chans :], 1)
    )


def split(block):
    high = block.astype(BF16)
    return high, (block - high.astype(F32)).astype(BF16)


def pairs_of(shape, across):
    rows = lax.broadcasted_iota(jnp.int32, shape, 0)
    columns = lax.broadcasted_iota(jnp.int32, shape, 1)
    hit = (rows // 2 == columns) if across == 0 else (columns // 2 == rows)
    return jnp.where(hit, 1.0, 0.0).astype(BF16)


def first_rows(vol_pad, w1, bias, pooled, mask, start, stop):
    gather = pairs_of((256, 128), 0)

    def row(y2, carry):
        total = jnp.zeros((64, 256), F32)
        for x in range(2):
            for j in range(2):
                y = 2 * y2 + j
                cells = vol_pad[pl.ds(x, 3), pl.ds(y, 3)].reshape(288, 256)
                pre = combine(jnp.dot(w1[0:192, 0:288], cells, preferred_element_type=F32), 64) + bias
                mask[x, y] = jnp.where(pre > 0, 1.0, 0.0).astype(BF16)
                total = total + jnp.where(pre > 0, pre, 0.3 * pre)
        high, low = split(total)
        summed = jnp.dot(high, gather, preferred_element_type=F32) + jnp.dot(
            low, gather, preferred_element_type=F32
        )
        pooled[0, y2] = (summed * 0.125).astype(BF16)
        return carry

    lax.fori_loop(start, stop, row, 0)


def two_rows(ref, y, chans):
    return jnp.concatenate(
        [ref[:, pl.ds(y + j, 3)].reshape(9 * chans, 128) for j in range(2)], axis=1
    )


def across(a, b):
    return lax.dot_general(a, b, (((1,), (1,)), ((), ())), preferred_element_type=F32)


def back_rows(vol_pad, cot_pad, wbt, mask, gw1):
    spread = pairs_of((128, 256), 1)
    ones = jnp.ones((16, 1024), BF16)

    def pair(step, carry):
        y2 = 2 * step
        stacked = jnp.dot(wbt[...], two_rows(cot_pad, y2, 128), preferred_element_type=F32)
        for j in range(2):
            back = combine(stacked[:, 128 * j : 128 * (j + 1)], 64) * 0.125
            high, low = split(back)
            wide = jnp.dot(high, spread, preferred_element_type=F32) + jnp.dot(
                low, spread, preferred_element_type=F32
            )
            grads, fields = [], []
            for x in range(2):
                for i in range(2):
                    y = 2 * (y2 + j) + i
                    kept = mask[x, y].astype(F32)
                    grad = jnp.where(kept > 0, wide, 0.3 * wide)
                    grads.append(
                        jnp.concatenate([shifted(grad, 1), grad, shifted(grad, -1)], axis=0).astype(BF16)
                    )
                    fields.append(vol_pad[pl.ds(x, 3), pl.ds(y, 3)].reshape(288, 256))
            cells = jnp.concatenate([jnp.concatenate(fields, axis=1), ones], axis=0)
            gw1[0:304, 0:192] += across(cells, jnp.concatenate(grads, axis=1))
        return carry

    lax.fori_loop(0, 4, pair, 0)


def second_rows(cot_pad, wf_all, pool_pad, second):
    def pair(step, carry):
        y2 = 2 * step
        weights = wf_all[...].reshape(384, 640)[:, 0:576]
        stacked = jnp.dot(weights, two_rows(pool_pad, y2, 64), preferred_element_type=F32)
        for j in range(2):
            second[y2 + j] = combine(stacked[:, 128 * j : 128 * (j + 1)], 128).astype(BF16)
        return carry

    lax.fori_loop(0, 4, pair, 0)


def second_grads(cot_pad, pooled, gw2, plane):
    ones = jnp.ones((16, 256), BF16)

    def pair(step, carry):
        y2 = 2 * step
        own = []
        for j in range(2):
            cells = pooled[0, y2 + j].astype(F32)
            own.append(jnp.concatenate([shifted(cells, -1), cells, shifted(cells, 1)], axis=0).astype(BF16))
        fields = jnp.concatenate([jnp.concatenate(own, axis=1), ones], axis=0)
        cots = jnp.concatenate(
            [cot_pad[plane, pl.ds(y2 + j, 3)].reshape(384, 128) for j in range(2)], axis=1
        )
        gw2[384 * plane : 384 * plane + 384, 0:208] += across(cots, fields)
        return carry

    lax.fori_loop(0, 4, pair, 0)


def whole_kernel(
    vol, cot, k1, b1, k2, rows_out, whole2, all1,
    vol_src, cot_src, wf_own, vol_pad, cot_pad, wf_all, w1t, w1, wbt, pooled, pool_pad, mask, second, gw1, gw2,
    pack1, send1, recv1, sums1, last1, pack2, send2, early2, late2, part2, parts2,
    ls, vs, vr, cs, cr, fs, fr, ws, wr, xs, xr, ps, pr, os_, or_,
    s1, r1, t1, q1, g1, h1, s2, r2, s3, r3, t2, q2, g2, h2,
):
    sx, sy, rep = place()
    core = sx % 2
    left, right = (sx + 7) % 8, (sx + 1) % 8
    partner = (sx + 1 - 2 * core, sy, rep)
    peers = [(sx, (sy + d) % 8, rep) for d in range(1, 8)]
    column = [((sx + d) % 8, sy, rep) for d in range(1, 8)]
    group1, group2 = sy * 2 + rep, sx * 2 + rep
    mates1, mates2 = [], []
    for e in range(1, 16):
        other = (group1 + e) % 16
        mates1.append((sx, other // 2, other % 2))
        other = (group2 + e) % 16
        mates2.append((other // 2, sy, other % 2))
    mine = pl.ds(pl.multiple_of(16 * sy, 16), 16)

    def theirs(d):
        return pl.ds(pl.multiple_of(16 * ((sy + d) % 8), 16), 16)

    barrier = pltpu.get_barrier_semaphore()
    around = [((sx + (dx + 8)) % 8, (sy + (dy + 8)) % 8, rep) for dx in (-1, 1) for dy in (-1, 1)]
    opposite = [(sx, (sy + d) % 8, 1 - rep) for d in range(1, 8)]
    greeted = around + peers + opposite + mates2
    for device in greeted:
        pl.semaphore_signal(barrier, inc=1, device_id=device, device_id_type=MESH)
    vol_src[...] = jnp.stack([jnp.swapaxes(vol[:, x], 0, 1) for x in range(2)])
    cot_src[0] = jnp.zeros((16, 128), BF16)
    cot_src[65] = jnp.zeros((16, 128), BF16)
    cot_src[1:65] = jnp.swapaxes(cot[...], 0, 1)
    for k in range(9):
        for z in range(3):
            wf_own[z, :, 64 * k : 64 * k + 64] = k2[3 * k + z]
    wf_own[:, :, 576:640] = jnp.zeros((3, 16, 64), BF16)
    pl.semaphore_wait(barrier, len(greeted))
    halo = halo_copies(vol_src, vol_pad, vs, vr)
    for copy in halo:
        copy.start()
    order = (4, 1, 7, 3, 5, 2, 6)
    exchange = {}
    for d in order:
        source = cot_src.at[pl.ds(8 * ((sy + d) % 8), 10)]
        exchange[d] = remote(source, cot_pad.at[1, :, mine, :], cs.at[d], cr.at[d], peers[d - 1])
        exchange[d].start()
    planes = pl.ds(core, 2)
    own_cot = cot_src.at[pl.ds(8 * sy, 10)]
    locals_ = [
        pltpu.make_async_copy(vol_src, vol_pad.at[pl.ds(1, 2), pl.ds(1, 16)], ls.at[0]),
        pltpu.make_async_copy(own_cot, cot_pad.at[1, :, mine, :], ls.at[1]),
        pltpu.make_async_copy(wf_own, wf_all.at[:, mine, :], ls.at[2]),
    ]
    for copy in locals_:
        copy.start()
    forwards = []

    def forward(d):
        rows = theirs(8 - d)
        source = cot_pad.at[1, :, rows, :] if d else own_cot
        both = [
            remote(source, cot_pad.at[2, :, rows, :], fs.at[d], fr.at[d], (left, sy, rep)),
            remote(source, cot_pad.at[0, :, rows, :], fs.at[8 + d], fr.at[8 + d], (right, sy, rep)),
        ]
        for copy in both:
            copy.start()
        forwards.extend(both)

    forward(0)
    for k in range(9):
        for z in range(3):
            w1t[32 * k : 32 * k + 32, 64 * z : 64 * z + 64] = k1[3 * k + z]
    w1t[288:384, :] = jnp.zeros((96, 256), BF16)
    w1t[0:288, 192:256] = jnp.zeros((288, 64), BF16)
    w1[...] = w1t[...].T
    square = (64, 64)
    diagonal = lax.broadcasted_iota(jnp.int32, square, 0) == lax.broadcasted_iota(jnp.int32, square, 1)
    bias = jnp.sum(jnp.where(diagonal, b1[...], 0.0), axis=1, keepdims=True)
    gw1[...] = jnp.zeros_like(gw1)
    gw2[...] = jnp.zeros_like(gw2)
    pack1[28:32] = jnp.zeros((4, 16, 128), F32)
    pack2[5] = jnp.zeros((128, 128), F32)
    pack2[15] = jnp.zeros((128, 128), F32)
    for copy in locals_ + halo:
        copy.wait()
    clear_rim(vol_pad)
    first_rows(vol_pad, w1, bias, pooled, mask, 0, 1)
    for d in order[:5]:
        exchange[d].wait_recv()
        forward(d)
    weights = {}
    for d in order:
        weights[d] = remote(wf_own.at[planes], wf_all.at[planes, mine, :], ws.at[d], wr.at[d], peers[d - 1])
        weights[d].start()
    first_rows(vol_pad, w1, bias, pooled, mask, 1, 2)
    for d in order[5:]:
        exchange[d].wait_recv()
        forward(d)
    first_rows(vol_pad, w1, bias, pooled, mask, 2, 8)
    pool_halo = halo_copies(pooled, pool_pad, ps, pr)
    for copy in pool_halo:
        copy.start()
    pool_pad[1, 1:9] = pooled[0]
    second_grads(cot_pad, pooled, gw2, 1)

    def taps(plane, row, low, high):
        at = 384 * plane + 128 * row
        return gw2[at : at + 128, low:high]

    def both(one, other):
        return jnp.concatenate([one, other], axis=1)

    for j in range(3):
        pack2[j] = taps(1, j, 0, 128)
    pack2[3] = both(taps(1, 0, 128, 192), taps(1, 1, 128, 192))
    pack2[4] = both(taps(1, 2, 128, 192), taps(1, 1, 192, 256))
    send2[0:6] = pack2[0:6].astype(BF16)
    first2 = []

    def exchange2(start, count, landing, send, recv):
        for e in range(1, 16):
            other = (group1 + e) % 16
            slots = pl.ds(start + count * (other % 2), count)
            rows = pl.ds(pl.multiple_of(16 * (other // 2), 16), 16)
            first2.append(
                remote(send2.at[slots, rows, :], landing.at[e], send.at[e], recv.at[e], mates1[e - 1])
            )
            first2[-1].start()

    exchange2(0, 3, early2, s2, r2)
    share = []
    plane = pl.ds(2 * core, 1)
    for d in order:
        weights[d].wait_recv()
        rows = theirs(8 - d)
        share.append(
            remote(wf_all.at[plane, rows, :], wf_all.at[plane, rows, :], xs.at[d], xr.at[d], partner)
        )
        share[-1].start()
    for copy in forwards:
        copy.wait()

    @pl.when(sx == 0)
    def _():
        cot_pad[0] = jnp.zeros(cot_pad.shape[1:], BF16)

    @pl.when(sx == 7)
    def _():
        cot_pad[2] = jnp.zeros(cot_pad.shape[1:], BF16)

    second_grads(cot_pad, pooled, gw2, 0)
    second_grads(cot_pad, pooled, gw2, 2)
    for j in range(3):
        pack2[6 + j] = taps(0, j, 0, 128)
        pack2[9 + j] = taps(2, j, 0, 128)
    pack2[12] = both(taps(0, 0, 128, 192), taps(0, 1, 128, 192))
    pack2[13] = both(taps(0, 2, 128, 192), taps(2, 0, 128, 192))
    pack2[14] = both(taps(2, 1, 128, 192), taps(2, 2, 128, 192))
    send2[6:16] = pack2[6:16].astype(BF16)
    exchange2(6, 5, late2, s3, r3)
    for copy in share:
        copy.wait()
    for d in order:
        exchange[d].wait_send()
        weights[d].wait_send()
    for z in range(3):
        turned = wf_all[z].T
        for k in range(9):
            wbt[64 * (2 - z) : 64 * (3 - z), 128 * (8 - k) : 128 * (9 - k)] = turned[64 * k : 64 * k + 64]
    back_rows(vol_pad, cot_pad, wbt, mask, gw1)
    for i in range(18):
        pack1[i] = gw1[16 * i : 16 * (i + 1), 0:128]
    for i in range(9):
        pack1[18 + i] = jnp.concatenate(
            [gw1[16 * i : 16 * (i + 1), 128:192], gw1[144 + 16 * i : 160 + 16 * i, 128:192]], axis=1
        )
    pack1[27] = gw1[288:304, 0:128]
    send1[...] = pack1[...].astype(BF16)
    first1 = []
    for e in range(1, 16):
        rows = pl.ds(2 * ((group1 + e) % 16), 2)
        first1.append(remote(send1.at[rows], recv1.at[e], s1.at[e], r1.at[e], mates1[e - 1]))
    for copy in first1:
        copy.start()
    for copy in pool_halo:
        copy.wait()
    clear_rim(pool_pad)
    second_rows(cot_pad, wf_all, pool_pad, second)
    here = pl.ds(pl.multiple_of(8 * sy, 8), 8)
    outs = []
    for d in order:
        outs.append(remote(second.at[:, theirs(d), :], rows_out.at[here], os_.at[d], or_.at[d], peers[d - 1]))
    kept = pltpu.make_async_copy(second.at[:, mine, :], rows_out.at[here], ls.at[3])
    for copy in first2:
        copy.wait()
    here2 = pack2[pl.ds(3 * rep, 3), mine, :]
    there2 = pack2[pl.ds(6 + 5 * rep, 5), mine, :]
    for e in range(1, 16):
        here2 = here2 + early2[e].astype(F32)
        there2 = there2 + late2[e].astype(F32)
    for i in range(8):
        for h in range(2):
            part2[2 * i + h] = (here2[i] if i < 3 else there2[i - 3])[8 * h : 8 * h + 8]
    reduce2 = []
    for d in range(1, 8):
        rows = pl.ds(2 * ((sx + d) % 8), 2)
        reduce2.append(remote(part2.at[rows], parts2.at[d], t2.at[d], q2.at[d], column[d - 1]))
    for copy in reduce2 + outs + [kept]:
        copy.start()
    for copy in first1:
        copy.wait()
    sum1 = pack1[pl.ds(2 * group1, 2)]
    for e in range(1, 16):
        sum1 = sum1 + recv1[e].astype(F32)
    sums1[sx] = sum1
    reduce1 = []
    for d in range(1, 8):
        reduce1.append(remote(sums1.at[sx], sums1.at[sx], t1.at[d], q1.at[d], column[d - 1]))
    for copy in reduce1:
        copy.start()
    for copy in reduce2:
        copy.wait()
    own = pl.ds(2 * sx, 2)
    total2 = part2[own]
    for d in range(1, 8):
        total2 = total2 + parts2[d]
    whole2[rep, own] = total2
    gather2 = []
    for e in range(1, 16):
        gather2.append(
            remote(whole2.at[rep, own], whole2.at[rep, own], g2.at[e], h2.at[e], mates2[e - 1])
        )
    for copy in gather2:
        copy.start()
    for copy in reduce1:
        copy.wait()
    total1 = sums1[0]
    for m in range(1, 8):
        total1 = total1 + sums1[m]
    last1[...] = total1.astype(BF16)
    slots = pl.ds(2 * group1, 2)
    gather1 = []
    for e in range(1, 16):
        gather1.append(remote(last1, all1.at[slots], g1.at[e], h1.at[e], mates1[e - 1]))
    for copy in gather1:
        copy.start()
    all1[slots] = total1.astype(BF16)
    kept.wait()
    for copy in outs + gather2 + gather1:
        copy.wait()


def final_kernel(scale, rows, whole2, all1, b2, second_out, gw2_out, gb2_out, gw1_out, gb1_out):
    square = (16, 16)
    diagonal = lax.broadcasted_iota(jnp.int32, square, 0) == lax.broadcasted_iota(jnp.int32, square, 1)
    bias = jnp.sum(jnp.where(diagonal, b2[...], 0.0), axis=1, keepdims=True)
    second_out[...] = jnp.swapaxes(rows[...].astype(F32) + bias[None], 0, 1)
    def tap(plane, row, z):
        return 3 * (8 - 3 * plane - row) + z

    low = {0: (1, 0), 1: (1, 1), 2: (1, 2), 6: (0, 0), 7: (0, 1), 8: (0, 2), 9: (2, 0), 10: (2, 1), 11: (2, 2)}
    high = {3: ((1, 0), (1, 1)), 4: ((1, 2), None), 12: ((0, 0), (0, 1)), 13: ((0, 2), (2, 0)), 14: ((2, 1), (2, 2))}
    parts = []
    for half in range(2):
        for i in range(8):
            slot = 3 * half + i if i < 3 else 6 + 5 * half + i - 3
            for h in range(2):
                at = slice(8 * h, 8 * h + 8)
                tile = whole2[half, 2 * i + h] * scale
                if slot in low:
                    gw2_out[tap(*low[slot], 0), at, :] = tile[:, 0:64]
                    gw2_out[tap(*low[slot], 1), at, :] = tile[:, 64:128]
                elif slot in high:
                    one, other = high[slot]
                    gw2_out[tap(*one, 2), at, :] = tile[:, 0:64]
                    if other:
                        gw2_out[tap(*other, 2), at, :] = tile[:, 64:128]
                    else:
                        parts.append(tile[:, 64:65])
    gb2_out[...] = jnp.sum(jnp.where(diagonal, jnp.concatenate(parts, axis=0), 0.0), axis=0, keepdims=True)
    for i in range(27):
        block = all1[i].astype(F32) * scale
        for h in range(2):
            tile = block[8 * h : 8 * h + 8]
            if i < 18:
                at = 16 * i + 8 * h
                for z in range(2):
                    gw1_out[3 * (at // 32) + z, at % 32 : at % 32 + 8, :] = tile[:, 64 * z : 64 * z + 64]
            else:
                for z in range(2):
                    at = 144 * z + 16 * (i - 18) + 8 * h
                    gw1_out[3 * (at // 32) + 2, at % 32 : at % 32 + 8, :] = tile[:, 64 * z : 64 * z + 64]
    gb1_out[...] = all1[27].astype(F32)[0:1, 64:128] * scale


def dma(n):
    return pltpu.SemaphoreType.DMA((n,))


def per_device(volume, first_kernel, first_bias, second_kernel, second_bias, cotangent):
    scale = 1.0 / math.sqrt(131072)
    k1 = first_kernel.transpose(2, 3, 4, 1, 0).reshape(27, 32, 64)
    k2 = second_kernel.transpose(2, 3, 4, 0, 1).reshape(27, 16, 64)
    outs = [((64, 16, 128), BF16), ((2, 16, 8, 128), F32), ((32, 16, 128), BF16)]
    scratch = [
        ((2, 16, 32, 256), BF16),
        ((66, 16, 128), BF16),
        ((3, 16, 640), BF16),
        ((4, 18, 32, 256), BF16),
        ((3, 10, 128, 128), BF16),
        ((3, 128, 640), BF16),
        ((384, 256), BF16),
        ((256, 384), BF16),
        ((192, 1152), BF16),
        ((1, 8, 64, 128), BF16),
        ((3, 10, 64, 128), BF16),
        ((2, 16, 64, 256), BF16),
        ((8, 128, 128), BF16),
        ((304, 256), F32),
        ((1152, 256), F32),
        ((32, 16, 128), F32),
        ((32, 16, 128), BF16),
        ((16, 2, 16, 128), BF16),
        ((8, 2, 16, 128), F32),
        ((2, 16, 128), BF16),
        ((16, 128, 128), F32),
        ((16, 128, 128), BF16),
        ((16, 3, 16, 128), BF16),
        ((16, 5, 16, 128), BF16),
        ((16, 8, 128), F32),
        ((8, 2, 8, 128), F32),
    ]
    sems = [4] + [8] * 4 + [16] * 2 + [8] * 8 + [16] * 2 + [8] * 2 + [16] * 6 + [8] * 2 + [16] * 2
    rows, whole2, all1 = pl.pallas_call(
        whole_kernel,
        out_shape=tuple(jax.ShapeDtypeStruct(s, t) for s, t in outs),
        in_specs=[VMEM] * 5,
        out_specs=tuple([VMEM] * 3),
        scratch_shapes=[pltpu.VMEM(s, t) for s, t in scratch] + [dma(n) for n in sems],
        compiler_params=pltpu.CompilerParams(
            vmem_limit_bytes=LIMIT, collective_id=0, has_side_effects=True
        ),
    )(volume[0], cotangent[0, :, 0], k1, first_bias[None], k2)
    finals = [((16, 64, 128), F32), ((27, 16, 64), F32), ((1, 16), F32), ((27, 32, 64), F32), ((1, 64), F32)]
    second_out, gw2, gb2, gw1, gb1 = pl.pallas_call(
        functools.partial(final_kernel, scale),
        out_shape=tuple(jax.ShapeDtypeStruct(s, t) for s, t in finals),
        in_specs=[VMEM] * 4,
        out_specs=tuple([VMEM] * 5),
        compiler_params=pltpu.CompilerParams(vmem_limit_bytes=LIMIT),
    )(rows, whole2, all1, second_bias[None])
    return (
        second_out[None, :, None],
        gw1.reshape(3, 3, 3, 32, 64).transpose(4, 3, 0, 1, 2),
        gb1[0],
        gw2.reshape(3, 3, 3, 16, 64).transpose(3, 4, 0, 1, 2),
        gb2[0],
    )


def solution(mesh):
    placed = (
        P("rep", None, "sx", "sy", None),
        P(),
        P(),
        P("sy", None, None, None, None),
        P("sy"),
        P("rep", "sy", "sx", None, None),
    )
    return jax.shard_map(
        per_device,
        mesh=mesh,
        in_specs=placed,
        out_specs=(
            P("rep", "sy", "sx", None, None),
            P(),
            P(),
            P("sy", None, None, None, None),
            P("sy"),
        ),
        check_vma=False,
    )
```

```python
import functools
import math

import jax
import jax.numpy as jnp
from jax import lax
from jax.experimental import pallas as pl
from jax.experimental.pallas import tpu as pltpu
from jax.sharding import PartitionSpec as P

MESH = pl.DeviceIdType.MESH
BF16 = jnp.bfloat16
F32 = jnp.float32
NEIGHBOURS = [(dx, dy) for dx in (-1, 0, 1) for dy in (-1, 0, 1) if (dx, dy) != (0, 0)]
VMEM = pl.BlockSpec(memory_space=pltpu.VMEM)
LIMIT = 60 * 1024 * 1024


def place():
    return lax.axis_index("sx"), lax.axis_index("sy"), lax.axis_index("rep")


def remote(src, dst, send, recv, device):
    return pltpu.make_async_remote_copy(
        src_ref=src, dst_ref=dst, send_sem=send, recv_sem=recv, device_id=device, device_id_type=MESH
    )


def halo_copies(src, dst, send, recv):
    sx, sy, rep = place()
    cells_x, cells_y = src.shape[0], src.shape[1]
    rim_x, rim_y = cells_x + 1, cells_y + 1
    copies = []
    for k, (dx, dy) in enumerate(NEIGHBOURS):
        from_x = {1: pl.ds(cells_x - 1, 1), -1: pl.ds(0, 1), 0: pl.ds(0, cells_x)}[dx]
        from_y = {1: pl.ds(cells_y - 1, 1), -1: pl.ds(0, 1), 0: pl.ds(0, cells_y)}[dy]
        to_x = {1: pl.ds(0, 1), -1: pl.ds(rim_x, 1), 0: pl.ds(1, cells_x)}[dx]
        to_y = {1: pl.ds(0, 1), -1: pl.ds(rim_y, 1), 0: pl.ds(1, cells_y)}[dy]
        device = ((sx + (dx + 8)) % 8, (sy + (dy + 8)) % 8, rep)
        copies.append(remote(src.at[from_x, from_y], dst.at[to_x, to_y], send.at[k], recv.at[k], device))
    return copies


def clear_rim(dst):
    sx, sy, _ = place()
    rim_x, rim_y = dst.shape[0] - 1, dst.shape[1] - 1

    @pl.when(sx == 0)
    def _():
        dst[0] = jnp.zeros(dst.shape[1:], dst.dtype)

    @pl.when(sx == 7)
    def _():
        dst[rim_x] = jnp.zeros(dst.shape[1:], dst.dtype)

    @pl.when(sy == 0)
    def _():
        dst[:, 0] = jnp.zeros((dst.shape[0],) + dst.shape[2:], dst.dtype)

    @pl.when(sy == 7)
    def _():
        dst[:, rim_y] = jnp.zeros((dst.shape[0],) + dst.shape[2:], dst.dtype)


def settle(region, *semaphores):
    for semaphore in semaphores:
        pltpu.make_async_copy(region, region, semaphore).wait()


def shifted(block, step):
    width = block.shape[-1]
    lanes = lax.broadcasted_iota(jnp.int32, block.shape, block.ndim - 1)
    if step == 1:
        return jnp.where(lanes == width - 1, 0.0, pltpu.roll(block, width - 1, block.ndim - 1))
    return jnp.where(lanes == 0, 0.0, pltpu.roll(block, 1, block.ndim - 1))


def combine(stacked, chans):
    return (
        stacked[chans : 2 * chans] + shifted(stacked[:chans], -1) + shifted(stacked[2 * chans :], 1)
    )


def split(block):
    high = block.astype(BF16)
    return high, (block - high.astype(F32)).astype(BF16)


def pairs_of(shape, across):
    rows = lax.broadcasted_iota(jnp.int32, shape, 0)
    columns = lax.broadcasted_iota(jnp.int32, shape, 1)
    hit = (rows // 2 == columns) if across == 0 else (columns // 2 == rows)
    return jnp.where(hit, 1.0, 0.0).astype(BF16)


def first_rows(vol_pad, w1, bias, pooled, mask, start, stop):
    gather = pairs_of((256, 128), 0)

    def row(y2, carry):
        total = jnp.zeros((64, 256), F32)
        for x in range(2):
            for j in range(2):
                y = 2 * y2 + j
                cells = vol_pad[pl.ds(x, 3), pl.ds(y, 3)].reshape(288, 256)
                pre = combine(jnp.dot(w1[0:192, 0:288], cells, preferred_element_type=F32), 64) + bias
                mask[x, y] = jnp.where(pre > 0, 1.0, 0.0).astype(BF16)
                total = total + jnp.where(pre > 0, pre, 0.3 * pre)
        high, low = split(total)
        summed = jnp.dot(high, gather, preferred_element_type=F32) + jnp.dot(
            low, gather, preferred_element_type=F32
        )
        pooled[0, y2] = (summed * 0.125).astype(BF16)
        return carry

    lax.fori_loop(start, stop, row, 0)


def two_rows(ref, y, chans):
    return jnp.concatenate(
        [ref[:, pl.ds(y + j, 3)].reshape(9 * chans, 128) for j in range(2)], axis=1
    )


def across(a, b):
    return lax.dot_general(a, b, (((1,), (1,)), ((), ())), preferred_element_type=F32)


def back_rows(vol_pad, cot_pad, wbt, mask, gw1):
    spread = pairs_of((128, 256), 1)
    ones = jnp.ones((16, 1024), BF16)

    def pair(step, carry):
        y2 = 2 * step
        stacked = jnp.dot(wbt[...], two_rows(cot_pad, y2, 128), preferred_element_type=F32)
        for j in range(2):
            back = combine(stacked[:, 128 * j : 128 * (j + 1)], 64) * 0.125
            high, low = split(back)
            wide = jnp.dot(high, spread, preferred_element_type=F32) + jnp.dot(
                low, spread, preferred_element_type=F32
            )
            grads, fields = [], []
            for x in range(2):
                for i in range(2):
                    y = 2 * (y2 + j) + i
                    kept = mask[x, y].astype(F32)
                    grad = jnp.where(kept > 0, wide, 0.3 * wide)
                    grads.append(
                        jnp.concatenate([shifted(grad, 1), grad, shifted(grad, -1)], axis=0).astype(BF16)
                    )
                    fields.append(vol_pad[pl.ds(x, 3), pl.ds(y, 3)].reshape(288, 256))
            cells = jnp.concatenate([jnp.concatenate(fields, axis=1), ones], axis=0)
            gw1[0:304, 0:192] += across(cells, jnp.concatenate(grads, axis=1))
        return carry

    lax.fori_loop(0, 4, pair, 0)


def second_rows(wlhs, pool_pad, second):
    def pair(step, carry):
        y2 = 2 * step
        stacked = jnp.dot(wlhs[...], two_rows(pool_pad, y2, 64), preferred_element_type=F32)
        for j in range(2):
            second[y2 + j] = combine(stacked[:, 128 * j : 128 * (j + 1)], 128).astype(BF16)
        return carry

    lax.fori_loop(0, 4, pair, 0)


def second_grads(cot_pad, pooled, gw2, plane):
    ones = jnp.ones((16, 256), BF16)

    def pair(step, carry):
        y2 = 2 * step
        own = []
        for j in range(2):
            cells = pooled[0, y2 + j].astype(F32)
            own.append(jnp.concatenate([shifted(cells, -1), cells, shifted(cells, 1)], axis=0).astype(BF16))
        fields = jnp.concatenate([jnp.concatenate(own, axis=1), ones], axis=0)
        cots = jnp.concatenate(
            [cot_pad[plane, pl.ds(y2 + j, 3)].reshape(384, 128) for j in range(2)], axis=1
        )
        gw2[384 * plane : 384 * plane + 384, 0:208] += across(cots, fields)
        return carry

    lax.fori_loop(0, 4, pair, 0)


def whole_kernel(
    vol_hbm, cot_hbm, k1_hbm, b1_hbm, k2_hbm, rows_out, whole2, all1,
    vol, cot, k1, b1, k2, vol_src, cot_src, wf_own, vol_pad, cot_pad, wf_all, wlhs, w1t, w1, wbt, pooled, pool_pad, mask, second, gw1, gw2,
    pack1, send1, recv1, half1, sums1, last1, pack2, send2, early2, late2, part2, parts2,
    ins, ls, vs, vr, cs, cr, fs, fr, ws, wr, xs, xr, ps, pr, os_, or_,
    s1, r1, t1, q1, g1, h1, s2, r2, s3, r3, t2, q2, g2, h2,
):
    sx, sy, rep = place()
    core = sx % 2
    left, right = (sx + 7) % 8, (sx + 1) % 8
    partner = (sx + 1 - 2 * core, sy, rep)
    peers = [(sx, (sy + d) % 8, rep) for d in range(1, 8)]
    column = [((sx + d) % 8, sy, rep) for d in range(1, 8)]
    group1, group2 = sy * 2 + rep, sx * 2 + rep
    mates1, mates2 = [], []
    for e in range(1, 16):
        other = (group1 + e) % 16
        mates1.append((sx, other // 2, other % 2))
        other = (group2 + e) % 16
        mates2.append((other // 2, sy, other % 2))
    mine = pl.ds(pl.multiple_of(16 * sy, 16), 16)

    def theirs(d):
        return pl.ds(pl.multiple_of(16 * ((sy + d) % 8), 16), 16)

    barrier = pltpu.get_barrier_semaphore()
    around = [((sx + (dx + 8)) % 8, (sy + (dy + 8)) % 8, rep) for dx in (-1, 1) for dy in (-1, 1)]
    opposite = [(sx, (sy + d) % 8, 1 - rep) for d in range(1, 8)]
    greeted = around + peers + opposite + mates2
    for device in greeted:
        pl.semaphore_signal(barrier, inc=1, device_id=device, device_id_type=MESH)
    loads = [
        pltpu.make_async_copy(src, dst, ins.at[i])
        for i, (src, dst) in enumerate(
            [(vol_hbm, vol), (cot_hbm, cot), (k2_hbm, k2), (k1_hbm, k1), (b1_hbm, b1)]
        )
    ]
    for copy in loads:
        copy.start()
    for copy in loads:
        copy.wait()
    vol_src[...] = jnp.stack([jnp.swapaxes(vol[:, x], 0, 1) for x in range(2)])
    cot_src[0] = jnp.zeros((16, 128), BF16)
    cot_src[65] = jnp.zeros((16, 128), BF16)
    cot_src[1:65] = jnp.swapaxes(cot[...], 0, 1)
    for p in range(27):
        z, k = p // 9, p % 9
        wf_own[p // 2, :, 64 * (p % 2) : 64 * (p % 2) + 64] = k2[3 * k + z]
    wf_own[13, :, 64:128] = jnp.zeros((16, 64), BF16)
    pl.semaphore_wait(barrier, len(greeted))
    halo = halo_copies(vol_src, vol_pad, vs, vr)
    for copy in halo:
        copy.start()
    order = (4, 1, 7, 3, 5, 2, 6)
    exchange = {}
    for d in order:
        source = cot_src.at[pl.ds(8 * ((sy + d) % 8), 10)]
        exchange[d] = remote(source, cot_pad.at[1, :, mine, :], cs.at[d], cr.at[d], peers[d - 1])
        exchange[d].start()
    half = pl.ds(7 * core, 7)
    own_cot = cot_src.at[pl.ds(8 * sy, 10)]
    locals_ = [
        pltpu.make_async_copy(vol_src, vol_pad.at[pl.ds(1, 2), pl.ds(1, 16)], ls.at[0]),
        pltpu.make_async_copy(own_cot, cot_pad.at[1, :, mine, :], ls.at[1]),
        pltpu.make_async_copy(wf_own, wf_all.at[:, mine, :], ls.at[2]),
    ]
    for copy in locals_:
        copy.start()
    forwards = []

    def forward(d):
        rows = theirs(8 - d)
        source = cot_pad.at[1, :, rows, :] if d else own_cot
        both = [
            remote(source, cot_pad.at[2, :, rows, :], fs.at[0], fr.at[0], (left, sy, rep)),
            remote(source, cot_pad.at[0, :, rows, :], fs.at[1], fr.at[1], (right, sy, rep)),
        ]
        for copy in both:
            copy.start()
        forwards.extend(both)

    forward(0)
    for k in range(9):
        for z in range(3):
            w1t[32 * k : 32 * k + 32, 64 * z : 64 * z + 64] = k1[3 * k + z]
    w1t[288:384, :] = jnp.zeros((96, 256), BF16)
    w1t[0:288, 192:256] = jnp.zeros((288, 64), BF16)
    w1[...] = w1t[...].T
    square = (64, 64)
    diagonal = lax.broadcasted_iota(jnp.int32, square, 0) == lax.broadcasted_iota(jnp.int32, square, 1)
    bias = jnp.sum(jnp.where(diagonal, b1[...], 0.0), axis=1, keepdims=True)
    gw1[...] = jnp.zeros_like(gw1)
    gw2[...] = jnp.zeros_like(gw2)
    pack1[28:32] = jnp.zeros((4, 16, 128), F32)
    pack2[5] = jnp.zeros((128, 128), F32)
    pack2[15] = jnp.zeros((128, 128), F32)
    for copy in locals_:
        copy.wait()
    for d in order[:5]:
        exchange[d].wait_recv()
        forward(d)
    for copy in halo:
        copy.wait()
    clear_rim(vol_pad)
    first_rows(vol_pad, w1, bias, pooled, mask, 0, 1)
    for d in order[5:]:
        exchange[d].wait_recv()
        forward(d)
    weights = {}
    for d in order:
        weights[d] = remote(wf_own.at[half], wf_all.at[half, mine, :], ws.at[0], wr.at[0], peers[d - 1])
        weights[d].start()
    first_rows(vol_pad, w1, bias, pooled, mask, 1, 8)
    pool_halo = halo_copies(pooled, pool_pad, ps, pr)
    for copy in pool_halo:
        copy.start()
    pool_pad[1, 1:9] = pooled[0]
    second_grads(cot_pad, pooled, gw2, 1)

    def taps(plane, row, low, high):
        at = 384 * plane + 128 * row
        return gw2[at : at + 128, low:high]

    def both(one, other):
        return jnp.concatenate([one, other], axis=1)

    for j in range(3):
        pack2[j] = taps(1, j, 0, 128)
    pack2[3] = both(taps(1, 0, 128, 192), taps(1, 1, 128, 192))
    pack2[4] = both(taps(1, 2, 128, 192), taps(1, 1, 192, 256))
    send2[0:6] = pack2[0:6].astype(BF16)
    first2 = []

    def exchange2(start, count, landing, send, recv):
        for e in range(1, 16):
            other = (group1 + e) % 16
            slots = pl.ds(start + count * (other % 2), count)
            rows = pl.ds(pl.multiple_of(16 * (other // 2), 16), 16)
            first2.append(
                remote(send2.at[slots, rows, :], landing.at[e], send.at[0], recv.at[0], mates1[e - 1])
            )
            first2[-1].start()

    exchange2(0, 3, early2, s2, r2)
    share = []
    settle(wf_all.at[half, pl.ds(0, 112), :], ws.at[0], wr.at[0])
    for d in order:
        rows = theirs(8 - d)
        share.append(
            remote(wf_all.at[half, rows, :], wf_all.at[half, rows, :], xs.at[0], xr.at[0], partner)
        )
        share[-1].start()
    for side in range(2):
        settle(cot_pad.at[2 - 2 * side], fs.at[side], fr.at[side])

    @pl.when(sx == 0)
    def _():
        cot_pad[0] = jnp.zeros(cot_pad.shape[1:], BF16)

    @pl.when(sx == 7)
    def _():
        cot_pad[2] = jnp.zeros(cot_pad.shape[1:], BF16)

    second_grads(cot_pad, pooled, gw2, 0)
    second_grads(cot_pad, pooled, gw2, 2)
    for j in range(3):
        pack2[6 + j] = taps(0, j, 0, 128)
        pack2[9 + j] = taps(2, j, 0, 128)
    pack2[12] = both(taps(0, 0, 128, 192), taps(0, 1, 128, 192))
    pack2[13] = both(taps(0, 2, 128, 192), taps(2, 0, 128, 192))
    pack2[14] = both(taps(2, 1, 128, 192), taps(2, 2, 128, 192))
    send2[6:16] = pack2[6:16].astype(BF16)
    exchange2(6, 5, late2, s3, r3)
    settle(wf_all.at[half, pl.ds(0, 112), :], xs.at[0], xr.at[0])
    for d in order:
        exchange[d].wait_send()
    for p in range(27):
        z, k = p // 9, p % 9
        turned = wf_all[p // 2].T if p % 2 == 0 else turned
        rows = slice(64 * (p % 2), 64 * (p % 2) + 64)
        wbt[64 * (2 - z) : 64 * (3 - z), 128 * (8 - k) : 128 * (9 - k)] = turned[rows]
    back_rows(vol_pad, cot_pad, wbt, mask, gw1)
    for i in range(18):
        pack1[i] = gw1[16 * i : 16 * (i + 1), 0:128]
    for i in range(9):
        pack1[18 + i] = jnp.concatenate(
            [gw1[16 * i : 16 * (i + 1), 128:192], gw1[144 + 16 * i : 160 + 16 * i, 128:192]], axis=1
        )
    pack1[27] = gw1[288:304, 0:128]
    send1[...] = pack1[...].astype(BF16)
    high, low = split(gw1[288:304, 0:128])
    rows = lax.broadcasted_iota(jnp.int32, (16, 128), 0)
    send1[27] = jnp.where(rows == 0, high.astype(F32), low.astype(F32)).astype(BF16)
    pack1[27] = jnp.where(rows == 0, gw1[288:304, 0:128], 0.0)
    first1 = []
    for d in range(1, 8):
        rows = pl.ds(4 * ((sx + d) % 8), 4)
        first1.append(remote(send1.at[rows], recv1.at[d], s1.at[0], r1.at[0], column[d - 1]))
    for copy in first1:
        copy.start()
    for copy in pool_halo:
        copy.wait()
    clear_rim(pool_pad)
    for p in range(27):
        z, k = p // 9, p % 9
        piece = wf_all[p // 2, :, 64 * (p % 2) : 64 * (p % 2) + 64]
        wlhs[128 * z : 128 * z + 128, 64 * k : 64 * k + 64] = piece
    second_rows(wlhs, pool_pad, second)
    here = pl.ds(pl.multiple_of(8 * sy, 8), 8)
    outs = []
    for d in order:
        outs.append(remote(second.at[:, theirs(d), :], rows_out.at[here], os_.at[0], or_.at[0], peers[d - 1]))
    kept = pltpu.make_async_copy(second.at[:, mine, :], rows_out.at[here], ls.at[3])
    lines = lax.broadcasted_iota(jnp.int32, (16, 128), 0)

    def rounded(total, buffer):
        buffer[...] = total.astype(BF16)

        @pl.when(sx == 6)
        def _():
            fold_high, fold_low = split(jnp.sum(total[3][0:2], axis=0, keepdims=True))
            buffer[3] = jnp.where(lines == 0, fold_high.astype(F32), fold_low.astype(F32)).astype(BF16)

    settle(recv1.at[pl.ds(1, 7)], s1.at[0], r1.at[0])
    sum1 = pack1[pl.ds(4 * sx, 4)]
    for d in range(1, 8):
        sum1 = sum1 + recv1[d].astype(F32)
    rounded(sum1, half1)
    reduce1 = []
    for e in range(1, 16):
        reduce1.append(remote(half1, sums1.at[group1], t1.at[0], q1.at[0], mates1[e - 1]))
    for copy in reduce1:
        copy.start()
    sums1[group1] = half1[...]
    for copy in outs + [kept]:
        copy.start()
    settle(early2.at[pl.ds(1, 15)], s2.at[0], r2.at[0])
    settle(late2.at[pl.ds(1, 15)], s3.at[0], r3.at[0])
    here2 = pack2[pl.ds(3 * rep, 3), mine, :]
    there2 = pack2[pl.ds(6 + 5 * rep, 5), mine, :]
    for e in range(1, 16):
        here2 = here2 + early2[e].astype(F32)
        there2 = there2 + late2[e].astype(F32)
    for i in range(8):
        for h in range(2):
            part2[2 * i + h] = (here2[i] if i < 3 else there2[i - 3])[8 * h : 8 * h + 8]
    reduce2 = []
    for d in range(1, 8):
        rows = pl.ds(2 * ((sx + d) % 8), 2)
        reduce2.append(remote(part2.at[rows], parts2.at[d], t2.at[0], q2.at[0], column[d - 1]))
    for copy in reduce2:
        copy.start()
    settle(parts2.at[pl.ds(1, 7)], t2.at[0], q2.at[0])
    own = pl.ds(2 * sx, 2)
    total2 = part2[own]
    for d in range(1, 8):
        total2 = total2 + parts2[d]
    whole2[rep, own] = total2
    gather2 = []
    for e in range(1, 16):
        gather2.append(
            remote(whole2.at[rep, own], whole2.at[rep, own], g2.at[0], h2.at[0], mates2[e - 1])
        )
    for copy in gather2:
        copy.start()
    settle(sums1.at[pl.ds(0, 15)], t1.at[0], q1.at[0])
    total1 = sums1[0].astype(F32)
    for m in range(1, 16):
        total1 = total1 + sums1[m].astype(F32)
    rounded(total1, last1)
    slots = pl.ds(4 * sx, 4)
    gather1 = []
    for d in range(1, 8):
        gather1.append(remote(last1, all1.at[slots], g1.at[0], h1.at[0], column[d - 1]))
    for copy in gather1:
        copy.start()
    all1[slots] = last1[...]
    kept.wait()
    settle(rows_out.at[pl.ds(0, 56)], os_.at[0], or_.at[0])
    settle(pack1.at[pl.ds(0, 15)], g2.at[0], h2.at[0])
    settle(all1.at[pl.ds(0, 28)], g1.at[0], h1.at[0])


def final_kernel(scale, rows, whole2, all1, b2, second_out, gw2_out, gb2_out, gw1_out, gb1_out):
    square = (16, 16)
    diagonal = lax.broadcasted_iota(jnp.int32, square, 0) == lax.broadcasted_iota(jnp.int32, square, 1)
    bias = jnp.sum(jnp.where(diagonal, b2[...], 0.0), axis=1, keepdims=True)
    second_out[...] = jnp.swapaxes(rows[...].astype(F32) + bias[None], 0, 1)
    def tap(plane, row, z):
        return 3 * (8 - 3 * plane - row) + z

    low = {0: (1, 0), 1: (1, 1), 2: (1, 2), 6: (0, 0), 7: (0, 1), 8: (0, 2), 9: (2, 0), 10: (2, 1), 11: (2, 2)}
    high = {3: ((1, 0), (1, 1)), 4: ((1, 2), None), 12: ((0, 0), (0, 1)), 13: ((0, 2), (2, 0)), 14: ((2, 1), (2, 2))}
    parts = []
    for half in range(2):
        for i in range(8):
            slot = 3 * half + i if i < 3 else 6 + 5 * half + i - 3
            for h in range(2):
                at = slice(8 * h, 8 * h + 8)
                tile = whole2[half, 2 * i + h] * scale
                if slot in low:
                    gw2_out[tap(*low[slot], 0), at, :] = tile[:, 0:64]
                    gw2_out[tap(*low[slot], 1), at, :] = tile[:, 64:128]
                elif slot in high:
                    one, other = high[slot]
                    gw2_out[tap(*one, 2), at, :] = tile[:, 0:64]
                    if other:
                        gw2_out[tap(*other, 2), at, :] = tile[:, 64:128]
                    else:
                        parts.append(tile[:, 64:65])
    gb2_out[...] = jnp.sum(jnp.where(diagonal, jnp.concatenate(parts, axis=0), 0.0), axis=0, keepdims=True)
    for i in range(27):
        block = all1[i].astype(F32) * scale
        for h in range(2):
            tile = block[8 * h : 8 * h + 8]
            if i < 18:
                at = 16 * i + 8 * h
                for z in range(2):
                    gw1_out[3 * (at // 32) + z, at % 32 : at % 32 + 8, :] = tile[:, 64 * z : 64 * z + 64]
            else:
                for z in range(2):
                    at = 144 * z + 16 * (i - 18) + 8 * h
                    gw1_out[3 * (at // 32) + 2, at % 32 : at % 32 + 8, :] = tile[:, 64 * z : 64 * z + 64]
    gb1_out[...] = jnp.sum(all1[27].astype(F32)[0:2, 64:128], axis=0, keepdims=True) * scale


def dma(n):
    return pltpu.SemaphoreType.DMA((n,))


def per_device(volume, first_kernel, first_bias, second_kernel, second_bias, cotangent):
    scale = 1.0 / math.sqrt(131072)
    k1 = first_kernel.transpose(2, 3, 4, 1, 0).reshape(27, 32, 64)
    k2 = second_kernel.transpose(2, 3, 4, 0, 1).reshape(27, 16, 64)
    outs = [((64, 16, 128), BF16), ((2, 16, 8, 128), F32), ((32, 16, 128), BF16)]
    scratch = [
        ((32, 2, 16, 256), BF16),
        ((16, 64, 128), BF16),
        ((27, 32, 64), BF16),
        ((1, 64), F32),
        ((27, 16, 64), BF16),
        ((2, 16, 32, 256), BF16),
        ((66, 16, 128), BF16),
        ((14, 16, 128), BF16),
        ((4, 18, 32, 256), BF16),
        ((3, 10, 128, 128), BF16),
        ((14, 128, 128), BF16),
        ((384, 576), BF16),
        ((384, 256), BF16),
        ((256, 384), BF16),
        ((192, 1152), BF16),
        ((1, 8, 64, 128), BF16),
        ((3, 10, 64, 128), BF16),
        ((2, 16, 64, 256), BF16),
        ((8, 128, 128), BF16),
        ((304, 256), F32),
        ((1152, 256), F32),
        ((32, 16, 128), F32),
        ((32, 16, 128), BF16),
        ((8, 4, 16, 128), BF16),
        ((4, 16, 128), BF16),
        ((16, 4, 16, 128), BF16),
        ((4, 16, 128), BF16),
        ((16, 128, 128), F32),
        ((16, 128, 128), BF16),
        ((16, 3, 16, 128), BF16),
        ((16, 5, 16, 128), BF16),
        ((16, 8, 128), F32),
        ((8, 2, 8, 128), F32),
    ]
    sems = [5, 4] + [8] * 4 + [2] * 2 + [1] * 4 + [8] * 2 + [1] * 16
    rows, whole2, all1 = pl.pallas_call(
        whole_kernel,
        out_shape=tuple(jax.ShapeDtypeStruct(s, t) for s, t in outs),
        in_specs=[pl.BlockSpec(memory_space=pl.ANY)] * 5,
        out_specs=tuple([VMEM] * 3),
        scratch_shapes=[pltpu.VMEM(s, t) for s, t in scratch] + [dma(n) for n in sems],
        compiler_params=pltpu.CompilerParams(
            vmem_limit_bytes=LIMIT, collective_id=0, has_side_effects=True
        ),
    )(volume[0], cotangent[0, :, 0], k1, first_bias[None], k2)
    finals = [((16, 64, 128), F32), ((27, 16, 64), F32), ((1, 16), F32), ((27, 32, 64), F32), ((1, 64), F32)]
    second_out, gw2, gb2, gw1, gb1 = pl.pallas_call(
        functools.partial(final_kernel, scale),
        out_shape=tuple(jax.ShapeDtypeStruct(s, t) for s, t in finals),
        in_specs=[VMEM] * 4,
        out_specs=tuple([VMEM] * 5),
        compiler_params=pltpu.CompilerParams(vmem_limit_bytes=LIMIT),
    )(rows, whole2, all1, second_bias[None])
    return (
        second_out[None, :, None],
        gw1.reshape(3, 3, 3, 32, 64).transpose(4, 3, 0, 1, 2),
        gb1[0],
        gw2.reshape(3, 3, 3, 16, 64).transpose(3, 4, 0, 1, 2),
        gb2[0],
    )


def solution(mesh):
    placed = (
        P("rep", None, "sx", "sy", None),
        P(),
        P(),
        P("sy", None, None, None, None),
        P("sy"),
        P("rep", "sy", "sx", None, None),
    )
    return jax.shard_map(
        per_device,
        mesh=mesh,
        in_specs=placed,
        out_specs=(
            P("rep", "sy", "sx", None, None),
            P(),
            P(),
            P("sy", None, None, None, None),
            P("sy"),
        ),
        check_vma=False,
    )
```

```python
import functools
import math

import jax
import jax.numpy as jnp
from jax import lax
from jax.experimental import pallas as pl
from jax.experimental.pallas import tpu as pltpu
from jax.sharding import PartitionSpec as P

MESH = pl.DeviceIdType.MESH
BF16 = jnp.bfloat16
F32 = jnp.float32
NEIGHBOURS = [(dx, dy) for dx in (-1, 0, 1) for dy in (-1, 0, 1) if (dx, dy) != (0, 0)]
VMEM = pl.BlockSpec(memory_space=pltpu.VMEM)
LIMIT = 60 * 1024 * 1024


def place():
    return lax.axis_index("sx"), lax.axis_index("sy"), lax.axis_index("rep")


def remote(src, dst, send, recv, device):
    return pltpu.make_async_remote_copy(
        src_ref=src, dst_ref=dst, send_sem=send, recv_sem=recv, device_id=device, device_id_type=MESH
    )


def halo_copies(src, dst, send, recv):
    sx, sy, rep = place()
    cells_x, cells_y = src.shape[0], src.shape[1]
    rim_x, rim_y = cells_x + 1, cells_y + 1
    copies = []
    for k, (dx, dy) in enumerate(NEIGHBOURS):
        from_x = {1: pl.ds(cells_x - 1, 1), -1: pl.ds(0, 1), 0: pl.ds(0, cells_x)}[dx]
        from_y = {1: pl.ds(cells_y - 1, 1), -1: pl.ds(0, 1), 0: pl.ds(0, cells_y)}[dy]
        to_x = {1: pl.ds(0, 1), -1: pl.ds(rim_x, 1), 0: pl.ds(1, cells_x)}[dx]
        to_y = {1: pl.ds(0, 1), -1: pl.ds(rim_y, 1), 0: pl.ds(1, cells_y)}[dy]
        device = (lax.rem(sx + (dx + 8), 8), lax.rem(sy + (dy + 8), 8), rep)
        copies.append(remote(src.at[from_x, from_y], dst.at[to_x, to_y], send.at[0], recv.at[0], device))
    return copies


def clear_rim(dst):
    sx, sy, _ = place()
    rim_x, rim_y = dst.shape[0] - 1, dst.shape[1] - 1

    @pl.when(sx == 0)
    def _():
        dst[0] = jnp.zeros(dst.shape[1:], dst.dtype)

    @pl.when(sx == 7)
    def _():
        dst[rim_x] = jnp.zeros(dst.shape[1:], dst.dtype)

    @pl.when(sy == 0)
    def _():
        dst[:, 0] = jnp.zeros((dst.shape[0],) + dst.shape[2:], dst.dtype)

    @pl.when(sy == 7)
    def _():
        dst[:, rim_y] = jnp.zeros((dst.shape[0],) + dst.shape[2:], dst.dtype)


def settle(region, *semaphores):
    for semaphore in semaphores:
        pltpu.make_async_copy(region, region, semaphore).wait()


def shifted(block, step):
    width = block.shape[-1]
    lanes = lax.broadcasted_iota(jnp.int32, block.shape, block.ndim - 1)
    if step == 1:
        return jnp.where(lanes == width - 1, 0.0, pltpu.roll(block, width - 1, block.ndim - 1))
    return jnp.where(lanes == 0, 0.0, pltpu.roll(block, 1, block.ndim - 1))


def combine(stacked, chans):
    return (
        stacked[chans : 2 * chans] + shifted(stacked[:chans], -1) + shifted(stacked[2 * chans :], 1)
    )


def split(block):
    high = block.astype(BF16)
    return high, (block - high.astype(F32)).astype(BF16)


def pairs_of(shape, across):
    rows = lax.broadcasted_iota(jnp.int32, shape, 0)
    columns = lax.broadcasted_iota(jnp.int32, shape, 1)
    hit = (rows // 2 == columns) if across == 0 else (columns // 2 == rows)
    return jnp.where(hit, 1.0, 0.0).astype(BF16)


def first_rows(vol_pad, w1, bias, pooled, mask, start, stop):
    gather = pairs_of((256, 128), 0)

    def row(y2, carry):
        total = jnp.zeros((64, 256), F32)
        for x in range(2):
            for j in range(2):
                y = 2 * y2 + j
                cells = vol_pad[pl.ds(x, 3), pl.ds(y, 3)].reshape(288, 256)
                pre = combine(jnp.dot(w1[0:192, 0:288], cells, preferred_element_type=F32), 64) + bias
                mask[x, y] = jnp.where(pre > 0, 1.0, 0.0).astype(BF16)
                total = total + jnp.where(pre > 0, pre, 0.3 * pre)
        high, low = split(total)
        summed = jnp.dot(high, gather, preferred_element_type=F32) + jnp.dot(
            low, gather, preferred_element_type=F32
        )
        pooled[0, y2] = (summed * 0.125).astype(BF16)
        return carry

    lax.fori_loop(start, stop, row, 0)


def two_rows(ref, y, chans):
    return jnp.concatenate(
        [ref[:, pl.ds(y + j, 3)].reshape(9 * chans, 128) for j in range(2)], axis=1
    )


def across(a, b):
    return lax.dot_general(a, b, (((1,), (1,)), ((), ())), preferred_element_type=F32)


def back_rows(vol_pad, cot_pad, wbt, mask, gw1):
    spread = pairs_of((128, 256), 1)
    ones = jnp.ones((16, 1024), BF16)

    def pair(step, carry):
        y2 = 2 * step
        stacked = jnp.dot(wbt[...], two_rows(cot_pad, y2, 128), preferred_element_type=F32)
        for j in range(2):
            back = combine(stacked[:, 128 * j : 128 * (j + 1)], 64) * 0.125
            high, low = split(back)
            wide = jnp.dot(high, spread, preferred_element_type=F32) + jnp.dot(
                low, spread, preferred_element_type=F32
            )
            grads, fields = [], []
            for x in range(2):
                for i in range(2):
                    y = 2 * (y2 + j) + i
                    kept = mask[x, y].astype(F32)
                    grad = jnp.where(kept > 0, wide, 0.3 * wide)
                    grads.append(
                        jnp.concatenate([shifted(grad, 1), grad, shifted(grad, -1)], axis=0).astype(BF16)
                    )
                    fields.append(vol_pad[pl.ds(x, 3), pl.ds(y, 3)].reshape(288, 256))
            cells = jnp.concatenate([jnp.concatenate(fields, axis=1), ones], axis=0)
            gw1[0:304, 0:192] += across(cells, jnp.concatenate(grads, axis=1))
        return carry

    lax.fori_loop(0, 4, pair, 0)


def second_rows(wlhs, pool_pad, second):
    def pair(step, carry):
        y2 = 2 * step
        stacked = jnp.dot(wlhs[...], two_rows(pool_pad, y2, 64), preferred_element_type=F32)
        for j in range(2):
            second[y2 + j] = combine(stacked[:, 128 * j : 128 * (j + 1)], 128).astype(BF16)
        return carry

    lax.fori_loop(0, 4, pair, 0)


def second_grads(cot_pad, pooled, gw2, plane):
    ones = jnp.ones((16, 256), BF16)

    def pair(step, carry):
        y2 = 2 * step
        own = []
        for j in range(2):
            cells = pooled[0, y2 + j].astype(F32)
            own.append(jnp.concatenate([shifted(cells, -1), cells, shifted(cells, 1)], axis=0).astype(BF16))
        fields = jnp.concatenate([jnp.concatenate(own, axis=1), ones], axis=0)
        cots = jnp.concatenate(
            [cot_pad[plane, pl.ds(y2 + j, 3)].reshape(384, 128) for j in range(2)], axis=1
        )
        gw2[384 * plane : 384 * plane + 384, 0:208] += across(cots, fields)
        return carry

    lax.fori_loop(0, 4, pair, 0)


def whole_kernel(
    vol_hbm, cot_hbm, k1_hbm, b1_hbm, k2_hbm, rows_out, whole2, all1,
    vol, cot, k1, b1, k2, vol_src, cot_src, wf_own, vol_pad, cot_pad, wf_all, wlhs, w1t, w1, wbt, pooled, pool_pad, mask, second, gw1, gw2,
    pack1, send1, recv1, half1, sums1, last1, pack2, send2, early2, late2, part2, parts2,
    ins, ls, vs, vr, cs, cr, fs, fr, ws, wr, xs, xr, ps, pr, os_, or_,
    s1, r1, t1, q1, g1, h1, s2, r2, s3, r3, t2, q2, g2, h2,
):
    sx, sy, rep = place()
    core = lax.rem(sx, 2)
    left, right = lax.rem(sx + 7, 8), lax.rem(sx + 1, 8)
    partner = (sx + 1 - 2 * core, sy, rep)
    peers = [(sx, lax.rem(sy + d, 8), rep) for d in range(1, 8)]
    column = [(lax.rem(sx + d, 8), sy, rep) for d in range(1, 8)]
    group1, group2 = sy * 2 + rep, sx * 2 + rep
    mates1, mates2 = [], []
    for e in range(1, 16):
        other = lax.rem(group1 + e, 16)
        mates1.append((sx, lax.div(other, 2), lax.rem(other, 2)))
        other = lax.rem(group2 + e, 16)
        mates2.append((lax.div(other, 2), sy, lax.rem(other, 2)))
    mine = pl.ds(pl.multiple_of(16 * sy, 16), 16)

    def theirs(d):
        return pl.ds(pl.multiple_of(16 * (lax.rem(sy + d, 8)), 16), 16)

    barrier = pltpu.get_barrier_semaphore()
    around = [(lax.rem(sx + (dx + 8), 8), lax.rem(sy + (dy + 8), 8), rep) for dx in (-1, 1) for dy in (-1, 1)]
    opposite = [(sx, lax.rem(sy + d, 8), 1 - rep) for d in range(1, 8)]
    greeted = around + peers + opposite + mates2
    for device in greeted:
        pl.semaphore_signal(barrier, inc=1, device_id=device, device_id_type=MESH)
    loads = [
        pltpu.make_async_copy(src, dst, ins.at[i])
        for i, (src, dst) in enumerate(
            [(vol_hbm, vol), (cot_hbm, cot), (k2_hbm, k2), (k1_hbm, k1), (b1_hbm, b1)]
        )
    ]
    for copy in loads:
        copy.start()
    for copy in loads:
        copy.wait()
    vol_src[...] = jnp.stack([jnp.swapaxes(vol[:, x], 0, 1) for x in range(2)])
    cot_src[0] = jnp.zeros((16, 128), BF16)
    cot_src[65] = jnp.zeros((16, 128), BF16)
    cot_src[1:65] = jnp.swapaxes(cot[...], 0, 1)
    for p in range(27):
        z, k = p // 9, p % 9
        wf_own[p // 2, :, 64 * (p % 2) : 64 * (p % 2) + 64] = k2[3 * k + z]
    wf_own[13, :, 64:128] = jnp.zeros((16, 64), BF16)
    pl.semaphore_wait(barrier, len(greeted))
    halo = halo_copies(vol_src, vol_pad, vs, vr)
    for copy in halo:
        copy.start()
    order = (4, 1, 7, 3, 5, 2, 6)
    exchange = {}
    for d in order:
        source = cot_src.at[pl.ds(8 * (lax.rem(sy + d, 8)), 10)]
        exchange[d] = remote(source, cot_pad.at[1, :, mine, :], cs.at[d], cr.at[d], peers[d - 1])
        exchange[d].start()
    half = pl.ds(7 * core, 7)
    own_cot = cot_src.at[pl.ds(8 * sy, 10)]
    locals_ = [
        pltpu.make_async_copy(vol_src, vol_pad.at[pl.ds(1, 2), pl.ds(1, 16)], ls.at[0]),
        pltpu.make_async_copy(own_cot, cot_pad.at[1, :, mine, :], ls.at[1]),
        pltpu.make_async_copy(wf_own, wf_all.at[:, mine, :], ls.at[2]),
    ]
    for copy in locals_:
        copy.start()
    forwards = []

    def forward(d):
        rows = theirs(8 - d)
        source = cot_pad.at[1, :, rows, :] if d else own_cot
        both = [
            remote(source, cot_pad.at[2, :, rows, :], fs.at[0], fr.at[0], (left, sy, rep)),
            remote(source, cot_pad.at[0, :, rows, :], fs.at[1], fr.at[1], (right, sy, rep)),
        ]
        for copy in both:
            copy.start()
        forwards.extend(both)

    forward(0)
    for k in range(9):
        for z in range(3):
            w1t[32 * k : 32 * k + 32, 64 * z : 64 * z + 64] = k1[3 * k + z]
    w1t[288:384, :] = jnp.zeros((96, 256), BF16)
    w1t[0:288, 192:256] = jnp.zeros((288, 64), BF16)
    w1[...] = w1t[...].T
    square = (64, 64)
    diagonal = lax.broadcasted_iota(jnp.int32, square, 0) == lax.broadcasted_iota(jnp.int32, square, 1)
    bias = jnp.sum(jnp.where(diagonal, b1[...], 0.0), axis=1, keepdims=True)
    gw1[...] = jnp.zeros_like(gw1)
    gw2[...] = jnp.zeros_like(gw2)
    pack1[28:32] = jnp.zeros((4, 16, 128), F32)
    pack2[5] = jnp.zeros((128, 128), F32)
    pack2[15] = jnp.zeros((128, 128), F32)
    for copy in locals_:
        copy.wait()
    for d in order[:5]:
        exchange[d].wait_recv()
        forward(d)
    settle(mask.at[pl.ds(0, 2), pl.ds(0, 10)], vs.at[0], vr.at[0])
    clear_rim(vol_pad)
    first_rows(vol_pad, w1, bias, pooled, mask, 0, 1)
    for d in order[5:]:
        exchange[d].wait_recv()
        forward(d)
    weights = {}
    for d in order:
        weights[d] = remote(wf_own.at[half], wf_all.at[half, mine, :], ws.at[0], wr.at[0], peers[d - 1])
        weights[d].start()
    first_rows(vol_pad, w1, bias, pooled, mask, 1, 8)
    pool_halo = halo_copies(pooled, pool_pad, ps, pr)
    for copy in pool_halo:
        copy.start()
    pool_pad[1, 1:9] = pooled[0]
    second_grads(cot_pad, pooled, gw2, 1)

    def taps(plane, row, low, high):
        at = 384 * plane + 128 * row
        return gw2[at : at + 128, low:high]

    def both(one, other):
        return jnp.concatenate([one, other], axis=1)

    for j in range(3):
        pack2[j] = taps(1, j, 0, 128)
    pack2[3] = both(taps(1, 0, 128, 192), taps(1, 1, 128, 192))
    pack2[4] = both(taps(1, 2, 128, 192), taps(1, 1, 192, 256))
    send2[0:6] = pack2[0:6].astype(BF16)
    first2 = []

    def exchange2(start, count, landing, send, recv):
        for e in range(1, 16):
            other = lax.rem(group1 + e, 16)
            slots = pl.ds(start + count * lax.rem(other, 2), count)
            rows = pl.ds(pl.multiple_of(16 * lax.div(other, 2), 16), 16)
            first2.append(
                remote(send2.at[slots, rows, :], landing.at[e], send.at[0], recv.at[0], mates1[e - 1])
            )
            first2[-1].start()

    exchange2(0, 3, early2, s2, r2)
    share = []
    settle(wf_all.at[half, pl.ds(0, 112), :], ws.at[0], wr.at[0])
    for d in order:
        rows = theirs(8 - d)
        share.append(
            remote(wf_all.at[half, rows, :], wf_all.at[half, rows, :], xs.at[0], xr.at[0], partner)
        )
        share[-1].start()
    for side in range(2):
        settle(cot_pad.at[2 - 2 * side], fs.at[side], fr.at[side])

    @pl.when(sx == 0)
    def _():
        cot_pad[0] = jnp.zeros(cot_pad.shape[1:], BF16)

    @pl.when(sx == 7)
    def _():
        cot_pad[2] = jnp.zeros(cot_pad.shape[1:], BF16)

    second_grads(cot_pad, pooled, gw2, 0)
    second_grads(cot_pad, pooled, gw2, 2)
    for j in range(3):
        pack2[6 + j] = taps(0, j, 0, 128)
        pack2[9 + j] = taps(2, j, 0, 128)
    pack2[12] = both(taps(0, 0, 128, 192), taps(0, 1, 128, 192))
    pack2[13] = both(taps(0, 2, 128, 192), taps(2, 0, 128, 192))
    pack2[14] = both(taps(2, 1, 128, 192), taps(2, 2, 128, 192))
    send2[6:16] = pack2[6:16].astype(BF16)
    exchange2(6, 5, late2, s3, r3)
    settle(wf_all.at[half, pl.ds(0, 112), :], xs.at[0], xr.at[0])
    for d in order:
        exchange[d].wait_send()
    for p in range(27):
        z, k = p // 9, p % 9
        turned = wf_all[p // 2].T if p % 2 == 0 else turned
        rows = slice(64 * (p % 2), 64 * (p % 2) + 64)
        wbt[64 * (2 - z) : 64 * (3 - z), 128 * (8 - k) : 128 * (9 - k)] = turned[rows]
    back_rows(vol_pad, cot_pad, wbt, mask, gw1)
    for i in range(18):
        pack1[i] = gw1[16 * i : 16 * (i + 1), 0:128]
    for i in range(9):
        pack1[18 + i] = jnp.concatenate(
            [gw1[16 * i : 16 * (i + 1), 128:192], gw1[144 + 16 * i : 160 + 16 * i, 128:192]], axis=1
        )
    pack1[27] = gw1[288:304, 0:128]
    send1[...] = pack1[...].astype(BF16)
    high, low = split(gw1[288:304, 0:128])
    rows = lax.broadcasted_iota(jnp.int32, (16, 128), 0)
    send1[27] = jnp.where(rows == 0, high.astype(F32), low.astype(F32)).astype(BF16)
    pack1[27] = jnp.where(rows == 0, gw1[288:304, 0:128], 0.0)
    first1 = []
    for d in range(1, 8):
        rows = pl.ds(4 * (lax.rem(sx + d, 8)), 4)
        first1.append(remote(send1.at[rows], recv1.at[d], s1.at[0], r1.at[0], column[d - 1]))
    for copy in first1:
        copy.start()
    settle(mask.at[0, pl.ds(0, 11)], ps.at[0], pr.at[0])
    clear_rim(pool_pad)
    for p in range(27):
        z, k = p // 9, p % 9
        piece = wf_all[p // 2, :, 64 * (p % 2) : 64 * (p % 2) + 64]
        wlhs[128 * z : 128 * z + 128, 64 * k : 64 * k + 64] = piece
    second_rows(wlhs, pool_pad, second)
    here = pl.ds(pl.multiple_of(8 * sy, 8), 8)
    outs = []
    for d in order:
        outs.append(remote(second.at[:, theirs(d), :], rows_out.at[here], os_.at[0], or_.at[0], peers[d - 1]))
    kept = pltpu.make_async_copy(second.at[:, mine, :], rows_out.at[here], ls.at[3])
    lines = lax.broadcasted_iota(jnp.int32, (16, 128), 0)

    def rounded(total, buffer):
        buffer[...] = total.astype(BF16)

        @pl.when(sx == 6)
        def _():
            fold_high, fold_low = split(jnp.sum(total[3][0:2], axis=0, keepdims=True))
            buffer[3] = jnp.where(lines == 0, fold_high.astype(F32), fold_low.astype(F32)).astype(BF16)

    settle(recv1.at[pl.ds(1, 7)], s1.at[0], r1.at[0])
    sum1 = pack1[pl.ds(4 * sx, 4)]
    for d in range(1, 8):
        sum1 = sum1 + recv1[d].astype(F32)
    rounded(sum1, half1)
    reduce1 = []
    for e in range(1, 16):
        reduce1.append(remote(half1, sums1.at[group1], t1.at[0], q1.at[0], mates1[e - 1]))
    for copy in reduce1:
        copy.start()
    sums1[group1] = half1[...]
    for copy in outs + [kept]:
        copy.start()
    settle(early2.at[pl.ds(1, 15)], s2.at[0], r2.at[0])
    settle(late2.at[pl.ds(1, 15)], s3.at[0], r3.at[0])
    here2 = pack2[pl.ds(3 * rep, 3), mine, :]
    there2 = pack2[pl.ds(6 + 5 * rep, 5), mine, :]
    for e in range(1, 16):
        here2 = here2 + early2[e].astype(F32)
        there2 = there2 + late2[e].astype(F32)
    for i in range(8):
        for h in range(2):
            part2[2 * i + h] = (here2[i] if i < 3 else there2[i - 3])[8 * h : 8 * h + 8]
    reduce2 = []
    for d in range(1, 8):
        rows = pl.ds(2 * (lax.rem(sx + d, 8)), 2)
        reduce2.append(remote(part2.at[rows], parts2.at[d], t2.at[0], q2.at[0], column[d - 1]))
    for copy in reduce2:
        copy.start()
    settle(parts2.at[pl.ds(1, 7)], t2.at[0], q2.at[0])
    own = pl.ds(2 * sx, 2)
    total2 = part2[own]
    for d in range(1, 8):
        total2 = total2 + parts2[d]
    whole2[rep, own] = total2
    gather2 = []
    for e in range(1, 16):
        gather2.append(
            remote(whole2.at[rep, own], whole2.at[rep, own], g2.at[0], h2.at[0], mates2[e - 1])
        )
    for copy in gather2:
        copy.start()
    settle(sums1.at[pl.ds(0, 15)], t1.at[0], q1.at[0])
    total1 = sums1[0].astype(F32)
    for m in range(1, 16):
        total1 = total1 + sums1[m].astype(F32)
    rounded(total1, last1)
    slots = pl.ds(4 * sx, 4)
    gather1 = []
    for d in range(1, 8):
        gather1.append(remote(last1, all1.at[slots], g1.at[0], h1.at[0], column[d - 1]))
    for copy in gather1:
        copy.start()
    all1[slots] = last1[...]
    kept.wait()
    settle(rows_out.at[pl.ds(0, 56)], os_.at[0], or_.at[0])
    settle(pack1.at[pl.ds(0, 15)], g2.at[0], h2.at[0])
    settle(all1.at[pl.ds(0, 28)], g1.at[0], h1.at[0])


def final_kernel(scale, rows, whole2, all1, b2, second_out, gw2_out, gb2_out, gw1_out, gb1_out):
    square = (16, 16)
    diagonal = lax.broadcasted_iota(jnp.int32, square, 0) == lax.broadcasted_iota(jnp.int32, square, 1)
    bias = jnp.sum(jnp.where(diagonal, b2[...], 0.0), axis=1, keepdims=True)
    second_out[...] = jnp.swapaxes(rows[...].astype(F32) + bias[None], 0, 1)
    def tap(plane, row, z):
        return 3 * (8 - 3 * plane - row) + z

    low = {0: (1, 0), 1: (1, 1), 2: (1, 2), 6: (0, 0), 7: (0, 1), 8: (0, 2), 9: (2, 0), 10: (2, 1), 11: (2, 2)}
    high = {3: ((1, 0), (1, 1)), 4: ((1, 2), None), 12: ((0, 0), (0, 1)), 13: ((0, 2), (2, 0)), 14: ((2, 1), (2, 2))}
    parts = []
    for half in range(2):
        for i in range(8):
            slot = 3 * half + i if i < 3 else 6 + 5 * half + i - 3
            for h in range(2):
                at = slice(8 * h, 8 * h + 8)
                tile = whole2[half, 2 * i + h] * scale
                if slot in low:
                    gw2_out[tap(*low[slot], 0), at, :] = tile[:, 0:64]
                    gw2_out[tap(*low[slot], 1), at, :] = tile[:, 64:128]
                elif slot in high:
                    one, other = high[slot]
                    gw2_out[tap(*one, 2), at, :] = tile[:, 0:64]
                    if other:
                        gw2_out[tap(*other, 2), at, :] = tile[:, 64:128]
                    else:
                        parts.append(tile[:, 64:65])
    gb2_out[...] = jnp.sum(jnp.where(diagonal, jnp.concatenate(parts, axis=0), 0.0), axis=0, keepdims=True)
    for i in range(27):
        block = all1[i].astype(F32) * scale
        for h in range(2):
            tile = block[8 * h : 8 * h + 8]
            if i < 18:
                at = 16 * i + 8 * h
                for z in range(2):
                    gw1_out[3 * (at // 32) + z, at % 32 : at % 32 + 8, :] = tile[:, 64 * z : 64 * z + 64]
            else:
                for z in range(2):
                    at = 144 * z + 16 * (i - 18) + 8 * h
                    gw1_out[3 * (at // 32) + 2, at % 32 : at % 32 + 8, :] = tile[:, 64 * z : 64 * z + 64]
    gb1_out[...] = jnp.sum(all1[27].astype(F32)[0:2, 64:128], axis=0, keepdims=True) * scale


def dma(n):
    return pltpu.SemaphoreType.DMA((n,))


def per_device(volume, first_kernel, first_bias, second_kernel, second_bias, cotangent):
    scale = 1.0 / math.sqrt(131072)
    k1 = first_kernel.transpose(2, 3, 4, 1, 0).reshape(27, 32, 64)
    k2 = second_kernel.transpose(2, 3, 4, 0, 1).reshape(27, 16, 64)
    outs = [((64, 16, 128), BF16), ((2, 16, 8, 128), F32), ((32, 16, 128), BF16)]
    scratch = [
        ((32, 2, 16, 256), BF16),
        ((16, 64, 128), BF16),
        ((27, 32, 64), BF16),
        ((1, 64), F32),
        ((27, 16, 64), BF16),
        ((2, 16, 32, 256), BF16),
        ((66, 16, 128), BF16),
        ((14, 16, 128), BF16),
        ((4, 18, 32, 256), BF16),
        ((3, 10, 128, 128), BF16),
        ((14, 128, 128), BF16),
        ((384, 576), BF16),
        ((384, 256), BF16),
        ((256, 384), BF16),
        ((192, 1152), BF16),
        ((1, 8, 64, 128), BF16),
        ((3, 10, 64, 128), BF16),
        ((2, 16, 64, 256), BF16),
        ((8, 128, 128), BF16),
        ((304, 256), F32),
        ((1152, 256), F32),
        ((32, 16, 128), F32),
        ((32, 16, 128), BF16),
        ((8, 4, 16, 128), BF16),
        ((4, 16, 128), BF16),
        ((16, 4, 16, 128), BF16),
        ((4, 16, 128), BF16),
        ((16, 128, 128), F32),
        ((16, 128, 128), BF16),
        ((16, 3, 16, 128), BF16),
        ((16, 5, 16, 128), BF16),
        ((16, 8, 128), F32),
        ((8, 2, 8, 128), F32),
    ]
    sems = [5, 4] + [1] * 2 + [8] * 2 + [2] * 2 + [1] * 22
    rows, whole2, all1 = pl.pallas_call(
        whole_kernel,
        out_shape=tuple(jax.ShapeDtypeStruct(s, t) for s, t in outs),
        in_specs=[pl.BlockSpec(memory_space=pl.ANY)] * 5,
        out_specs=tuple([VMEM] * 3),
        scratch_shapes=[pltpu.VMEM(s, t) for s, t in scratch] + [dma(n) for n in sems],
        compiler_params=pltpu.CompilerParams(
            vmem_limit_bytes=LIMIT, collective_id=0, has_side_effects=True
        ),
    )(volume[0], cotangent[0, :, 0], k1, first_bias[None], k2)
    finals = [((16, 64, 128), F32), ((27, 16, 64), F32), ((1, 16), F32), ((27, 32, 64), F32), ((1, 64), F32)]
    second_out, gw2, gb2, gw1, gb1 = pl.pallas_call(
        functools.partial(final_kernel, scale),
        out_shape=tuple(jax.ShapeDtypeStruct(s, t) for s, t in finals),
        in_specs=[VMEM] * 4,
        out_specs=tuple([VMEM] * 5),
        compiler_params=pltpu.CompilerParams(vmem_limit_bytes=LIMIT),
    )(rows, whole2, all1, second_bias[None])
    return (
        second_out[None, :, None],
        gw1.reshape(3, 3, 3, 32, 64).transpose(4, 3, 0, 1, 2),
        gb1[0],
        gw2.reshape(3, 3, 3, 16, 64).transpose(3, 4, 0, 1, 2),
        gb2[0],
    )


def solution(mesh):
    placed = (
        P("rep", None, "sx", "sy", None),
        P(),
        P(),
        P("sy", None, None, None, None),
        P("sy"),
        P("rep", "sy", "sx", None, None),
    )
    return jax.shard_map(
        per_device,
        mesh=mesh,
        in_specs=placed,
        out_specs=(
            P("rep", "sy", "sx", None, None),
            P(),
            P(),
            P("sy", None, None, None, None),
            P("sy"),
        ),
        check_vma=False,
    )
```

```python
import functools
import math

import jax
import jax.numpy as jnp
from jax import lax
from jax.experimental import pallas as pl
from jax.experimental.pallas import tpu as pltpu
from jax.sharding import PartitionSpec as P

MESH = pl.DeviceIdType.MESH
BF16 = jnp.bfloat16
F32 = jnp.float32
NEIGHBOURS = [(dx, dy) for dx in (-1, 0, 1) for dy in (-1, 0, 1) if (dx, dy) != (0, 0)]
VMEM = pl.BlockSpec(memory_space=pltpu.VMEM)
LIMIT = 60 * 1024 * 1024


def place():
    return lax.axis_index("sx"), lax.axis_index("sy"), lax.axis_index("rep")


def remote(src, dst, send, recv, device):
    return pltpu.make_async_remote_copy(
        src_ref=src, dst_ref=dst, send_sem=send, recv_sem=recv, device_id=device, device_id_type=MESH
    )


def halo_copies(src, dst, send, recv):
    sx, sy, rep = place()
    cells_x, cells_y = src.shape[0], src.shape[1]
    rim_x, rim_y = cells_x + 1, cells_y + 1
    copies = []
    for k, (dx, dy) in enumerate(NEIGHBOURS):
        from_x = {1: pl.ds(cells_x - 1, 1), -1: pl.ds(0, 1), 0: pl.ds(0, cells_x)}[dx]
        from_y = {1: pl.ds(cells_y - 1, 1), -1: pl.ds(0, 1), 0: pl.ds(0, cells_y)}[dy]
        to_x = {1: pl.ds(0, 1), -1: pl.ds(rim_x, 1), 0: pl.ds(1, cells_x)}[dx]
        to_y = {1: pl.ds(0, 1), -1: pl.ds(rim_y, 1), 0: pl.ds(1, cells_y)}[dy]
        device = (lax.rem(sx + (dx + 8), 8), lax.rem(sy + (dy + 8), 8), rep)
        copies.append(remote(src.at[from_x, from_y], dst.at[to_x, to_y], send.at[0], recv.at[0], device))
    return copies


def clear_rim(dst):
    sx, sy, _ = place()
    rim_x, rim_y = dst.shape[0] - 1, dst.shape[1] - 1

    @pl.when(sx == 0)
    def _():
        dst[0] = jnp.zeros(dst.shape[1:], dst.dtype)

    @pl.when(sx == 7)
    def _():
        dst[rim_x] = jnp.zeros(dst.shape[1:], dst.dtype)

    @pl.when(sy == 0)
    def _():
        dst[:, 0] = jnp.zeros((dst.shape[0],) + dst.shape[2:], dst.dtype)

    @pl.when(sy == 7)
    def _():
        dst[:, rim_y] = jnp.zeros((dst.shape[0],) + dst.shape[2:], dst.dtype)


def settle(region, *semaphores):
    for semaphore in semaphores:
        pltpu.make_async_copy(region, region, semaphore).wait()


def shifted(block, step):
    width = block.shape[-1]
    lanes = lax.broadcasted_iota(jnp.int32, block.shape, block.ndim - 1)
    if step == 1:
        return jnp.where(lanes == width - 1, 0.0, pltpu.roll(block, width - 1, block.ndim - 1))
    return jnp.where(lanes == 0, 0.0, pltpu.roll(block, 1, block.ndim - 1))


def combine(stacked, chans):
    return (
        stacked[chans : 2 * chans] + shifted(stacked[:chans], -1) + shifted(stacked[2 * chans :], 1)
    )


def split(block):
    high = block.astype(BF16)
    return high, (block - high.astype(F32)).astype(BF16)


def pairs_of(shape, across):
    rows = lax.broadcasted_iota(jnp.int32, shape, 0)
    columns = lax.broadcasted_iota(jnp.int32, shape, 1)
    hit = (rows // 2 == columns) if across == 0 else (columns // 2 == rows)
    return jnp.where(hit, 1.0, 0.0).astype(BF16)


def first_rows(vol_pad, w1, bias, pooled, mask, start, stop):
    gather = pairs_of((256, 128), 0)

    def row(y2, carry):
        total = jnp.zeros((64, 256), F32)
        for x in range(2):
            for j in range(2):
                y = 2 * y2 + j
                cells = vol_pad[pl.ds(x, 3), pl.ds(y, 3)].reshape(288, 256)
                pre = combine(jnp.dot(w1[0:192, 0:288], cells, preferred_element_type=F32), 64) + bias
                mask[x, y] = jnp.where(pre > 0, 1.0, 0.0).astype(BF16)
                total = total + jnp.where(pre > 0, pre, 0.3 * pre)
        high, low = split(total)
        summed = jnp.dot(high, gather, preferred_element_type=F32) + jnp.dot(
            low, gather, preferred_element_type=F32
        )
        pooled[0, y2] = (summed * 0.125).astype(BF16)
        return carry

    lax.fori_loop(start, stop, row, 0)


def two_rows(ref, y, chans):
    return jnp.concatenate(
        [ref[:, pl.ds(y + j, 3)].reshape(9 * chans, 128) for j in range(2)], axis=1
    )


def across(a, b):
    return lax.dot_general(a, b, (((1,), (1,)), ((), ())), preferred_element_type=F32)


def back_rows(vol_pad, cot_pad, wbt, mask, gw1):
    spread = pairs_of((128, 256), 1)
    ones = jnp.ones((16, 1024), BF16)

    def pair(step, carry):
        y2 = 2 * step
        stacked = jnp.dot(wbt[...], two_rows(cot_pad, y2, 128), preferred_element_type=F32)
        for j in range(2):
            back = combine(stacked[:, 128 * j : 128 * (j + 1)], 64) * 0.125
            high, low = split(back)
            wide = jnp.dot(high, spread, preferred_element_type=F32) + jnp.dot(
                low, spread, preferred_element_type=F32
            )
            grads, fields = [], []
            for x in range(2):
                for i in range(2):
                    y = 2 * (y2 + j) + i
                    kept = mask[x, y].astype(F32)
                    grad = jnp.where(kept > 0, wide, 0.3 * wide)
                    grads.append(
                        jnp.concatenate([shifted(grad, 1), grad, shifted(grad, -1)], axis=0).astype(BF16)
                    )
                    fields.append(vol_pad[pl.ds(x, 3), pl.ds(y, 3)].reshape(288, 256))
            cells = jnp.concatenate([jnp.concatenate(fields, axis=1), ones], axis=0)
            gw1[0:304, 0:192] += across(cells, jnp.concatenate(grads, axis=1))
        return carry

    lax.fori_loop(0, 4, pair, 0)


def second_rows(wlhs, pool_pad, second):
    def pair(step, carry):
        y2 = 2 * step
        stacked = jnp.dot(wlhs[...], two_rows(pool_pad, y2, 64), preferred_element_type=F32)
        for j in range(2):
            second[y2 + j] = combine(stacked[:, 128 * j : 128 * (j + 1)], 128).astype(BF16)
        return carry

    lax.fori_loop(0, 4, pair, 0)


def second_grads(cot_pad, pooled, gw2, plane):
    ones = jnp.ones((16, 256), BF16)

    def pair(step, carry):
        y2 = 2 * step
        own = []
        for j in range(2):
            cells = pooled[0, y2 + j].astype(F32)
            own.append(jnp.concatenate([shifted(cells, -1), cells, shifted(cells, 1)], axis=0).astype(BF16))
        fields = jnp.concatenate([jnp.concatenate(own, axis=1), ones], axis=0)
        cots = jnp.concatenate(
            [cot_pad[plane, pl.ds(y2 + j, 3)].reshape(384, 128) for j in range(2)], axis=1
        )
        gw2[384 * plane : 384 * plane + 384, 0:208] += across(cots, fields)
        return carry

    lax.fori_loop(0, 4, pair, 0)


def whole_kernel(
    vol_hbm, cot_hbm, k1_hbm, b1_hbm, k2_hbm, rows_out, whole2, all1,
    vol, cot, k1, b1, k2, vol_src, cot_src, wf_own, vol_pad, cot_pad, wf_all, wlhs, w1t, w1, wbt, pooled, pool_pad, mask, second, gw1, gw2,
    pack1, send1, recv1, half1, sums1, last1, pack2, send2, early2, late2, part2, parts2,
    ins, ls, vs, vr, cs, cr, fs, fr, ws, wr, xs, xr, ps, pr, os_, or_,
    s1, r1, t1, q1, g1, h1, s2, r2, s3, r3, t2, q2, g2, h2,
):
    sx, sy, rep = place()
    core = lax.rem(sx, 2)
    left, right = lax.rem(sx + 7, 8), lax.rem(sx + 1, 8)
    partner = (sx + 1 - 2 * core, sy, rep)
    peers = [(sx, lax.rem(sy + d, 8), rep) for d in range(1, 8)]
    column = [(lax.rem(sx + d, 8), sy, rep) for d in range(1, 8)]
    group1, group2 = sy * 2 + rep, sx * 2 + rep
    mates1, mates2 = [], []
    for e in range(1, 16):
        other = lax.rem(group1 + e, 16)
        mates1.append((sx, lax.div(other, 2), lax.rem(other, 2)))
        other = lax.rem(group2 + e, 16)
        mates2.append((lax.div(other, 2), sy, lax.rem(other, 2)))
    mine = pl.ds(pl.multiple_of(16 * sy, 16), 16)

    def theirs(d):
        return pl.ds(pl.multiple_of(16 * (lax.rem(sy + d, 8)), 16), 16)

    barrier = pltpu.get_barrier_semaphore()
    around = [(lax.rem(sx + (dx + 8), 8), lax.rem(sy + (dy + 8), 8), rep) for dx in (-1, 1) for dy in (-1, 1)]
    opposite = [(sx, lax.rem(sy + d, 8), 1 - rep) for d in range(1, 8)]
    greeted = around + peers + opposite + mates2
    for device in greeted:
        pl.semaphore_signal(barrier, inc=1, device_id=device, device_id_type=MESH)
    loads = [
        pltpu.make_async_copy(src, dst, ins.at[i])
        for i, (src, dst) in enumerate(
            [(vol_hbm, vol), (cot_hbm, cot), (k2_hbm, k2), (k1_hbm, k1), (b1_hbm, b1)]
        )
    ]
    for copy in loads:
        copy.start()
    for copy in loads:
        copy.wait()
    vol_src[...] = jnp.stack([jnp.swapaxes(vol[:, x], 0, 1) for x in range(2)])
    cot_src[0] = jnp.zeros((16, 128), BF16)
    cot_src[65] = jnp.zeros((16, 128), BF16)
    cot_src[1:65] = jnp.swapaxes(cot[...], 0, 1)
    for p in range(27):
        z, k = p // 9, p % 9
        wf_own[p // 2, :, 64 * (p % 2) : 64 * (p % 2) + 64] = k2[3 * k + z]
    wf_own[13, :, 64:128] = jnp.zeros((16, 64), BF16)
    pl.semaphore_wait(barrier, len(greeted))
    halo = halo_copies(vol_src, vol_pad, vs, vr)
    for copy in halo:
        copy.start()
    order = (4, 1, 7, 3, 5, 2, 6)
    exchange = {}
    for d in order:
        source = cot_src.at[pl.ds(8 * (lax.rem(sy + d, 8)), 10)]
        exchange[d] = remote(source, cot_pad.at[1, :, mine, :], cs.at[d], cr.at[d], peers[d - 1])
        exchange[d].start()
    half = pl.ds(7 * core, 7)
    own_cot = cot_src.at[pl.ds(8 * sy, 10)]
    locals_ = [
        pltpu.make_async_copy(vol_src, vol_pad.at[pl.ds(1, 2), pl.ds(1, 16)], ls.at[0]),
        pltpu.make_async_copy(own_cot, cot_pad.at[1, :, mine, :], ls.at[1]),
        pltpu.make_async_copy(wf_own, wf_all.at[:, mine, :], ls.at[2]),
    ]
    for copy in locals_:
        copy.start()
    forwards = []

    def forward(d):
        rows = theirs(8 - d)
        source = cot_pad.at[1, :, rows, :] if d else own_cot
        both = [
            remote(source, cot_pad.at[2, :, rows, :], fs.at[0], fr.at[0], (left, sy, rep)),
            remote(source, cot_pad.at[0, :, rows, :], fs.at[1], fr.at[1], (right, sy, rep)),
        ]
        for copy in both:
            copy.start()
        forwards.extend(both)

    forward(0)
    for k in range(9):
        for z in range(3):
            w1t[32 * k : 32 * k + 32, 64 * z : 64 * z + 64] = k1[3 * k + z]
    w1t[288:384, :] = jnp.zeros((96, 256), BF16)
    w1t[0:288, 192:256] = jnp.zeros((288, 64), BF16)
    w1[...] = w1t[...].T
    square = (64, 64)
    diagonal = lax.broadcasted_iota(jnp.int32, square, 0) == lax.broadcasted_iota(jnp.int32, square, 1)
    bias = jnp.sum(jnp.where(diagonal, b1[...], 0.0), axis=1, keepdims=True)
    gw1[...] = jnp.zeros_like(gw1)
    gw2[...] = jnp.zeros_like(gw2)
    pack1[28:32] = jnp.zeros((4, 16, 128), F32)
    pack2[5] = jnp.zeros((128, 128), F32)
    pack2[15] = jnp.zeros((128, 128), F32)
    for copy in locals_:
        copy.wait()
    for d in order[:3]:
        exchange[d].wait_recv()
        forward(d)
    settle(mask.at[pl.ds(0, 2), pl.ds(0, 10)], vs.at[0], vr.at[0])
    clear_rim(vol_pad)
    first_rows(vol_pad, w1, bias, pooled, mask, 0, 1)
    for d in order[3:]:
        exchange[d].wait_recv()
        forward(d)
    weights = {}
    for d in order:
        weights[d] = remote(wf_own.at[half], wf_all.at[half, mine, :], ws.at[0], wr.at[0], peers[d - 1])
        weights[d].start()
    first_rows(vol_pad, w1, bias, pooled, mask, 1, 8)
    pool_halo = halo_copies(pooled, pool_pad, ps, pr)
    for copy in pool_halo:
        copy.start()
    pool_pad[1, 1:9] = pooled[0]
    second_grads(cot_pad, pooled, gw2, 1)

    def taps(plane, row, low, high):
        at = 384 * plane + 128 * row
        return gw2[at : at + 128, low:high]

    def both(one, other):
        return jnp.concatenate([one, other], axis=1)

    for j in range(3):
        pack2[j] = taps(1, j, 0, 128)
    pack2[3] = both(taps(1, 0, 128, 192), taps(1, 1, 128, 192))
    pack2[4] = both(taps(1, 2, 128, 192), taps(1, 1, 192, 256))
    send2[0:6] = pack2[0:6].astype(BF16)
    first2 = []

    def exchange2(start, count, landing, send, recv):
        for e in range(1, 16):
            other = lax.rem(group1 + e, 16)
            slots = pl.ds(start + count * lax.rem(other, 2), count)
            rows = pl.ds(pl.multiple_of(16 * lax.div(other, 2), 16), 16)
            first2.append(
                remote(send2.at[slots, rows, :], landing.at[e], send.at[0], recv.at[0], mates1[e - 1])
            )
            first2[-1].start()

    exchange2(0, 3, early2, s2, r2)
    share = []
    settle(wf_all.at[half, pl.ds(0, 112), :], ws.at[0], wr.at[0])
    for d in order:
        rows = theirs(8 - d)
        share.append(
            remote(wf_all.at[half, rows, :], wf_all.at[half, rows, :], xs.at[0], xr.at[0], partner)
        )
        share[-1].start()
    for side in range(2):
        settle(cot_pad.at[2 - 2 * side], fs.at[side], fr.at[side])

    @pl.when(sx == 0)
    def _():
        cot_pad[0] = jnp.zeros(cot_pad.shape[1:], BF16)

    @pl.when(sx == 7)
    def _():
        cot_pad[2] = jnp.zeros(cot_pad.shape[1:], BF16)

    second_grads(cot_pad, pooled, gw2, 0)
    second_grads(cot_pad, pooled, gw2, 2)
    for j in range(3):
        pack2[6 + j] = taps(0, j, 0, 128)
        pack2[9 + j] = taps(2, j, 0, 128)
    pack2[12] = both(taps(0, 0, 128, 192), taps(0, 1, 128, 192))
    pack2[13] = both(taps(0, 2, 128, 192), taps(2, 0, 128, 192))
    pack2[14] = both(taps(2, 1, 128, 192), taps(2, 2, 128, 192))
    send2[6:16] = pack2[6:16].astype(BF16)
    exchange2(6, 5, late2, s3, r3)
    settle(wf_all.at[half, pl.ds(0, 112), :], xs.at[0], xr.at[0])
    for d in order:
        exchange[d].wait_send()
    for p in range(27):
        z, k = p // 9, p % 9
        turned = wf_all[p // 2].T if p % 2 == 0 else turned
        rows = slice(64 * (p % 2), 64 * (p % 2) + 64)
        wbt[64 * (2 - z) : 64 * (3 - z), 128 * (8 - k) : 128 * (9 - k)] = turned[rows]
    back_rows(vol_pad, cot_pad, wbt, mask, gw1)
    for i in range(18):
        pack1[i] = gw1[16 * i : 16 * (i + 1), 0:128]
    for i in range(9):
        pack1[18 + i] = jnp.concatenate(
            [gw1[16 * i : 16 * (i + 1), 128:192], gw1[144 + 16 * i : 160 + 16 * i, 128:192]], axis=1
        )
    pack1[27] = gw1[288:304, 0:128]
    send1[...] = pack1[...].astype(BF16)
    high, low = split(gw1[288:304, 0:128])
    rows = lax.broadcasted_iota(jnp.int32, (16, 128), 0)
    send1[27] = jnp.where(rows == 0, high.astype(F32), low.astype(F32)).astype(BF16)
    pack1[27] = jnp.where(rows == 0, gw1[288:304, 0:128], 0.0)
    first1 = []
    for d in range(1, 8):
        rows = pl.ds(4 * (lax.rem(sx + d, 8)), 4)
        first1.append(remote(send1.at[rows], recv1.at[d], s1.at[0], r1.at[0], column[d - 1]))
    for copy in first1:
        copy.start()
    settle(mask.at[0, pl.ds(0, 11)], ps.at[0], pr.at[0])
    clear_rim(pool_pad)
    for p in range(27):
        z, k = p // 9, p % 9
        piece = wf_all[p // 2, :, 64 * (p % 2) : 64 * (p % 2) + 64]
        wlhs[128 * z : 128 * z + 128, 64 * k : 64 * k + 64] = piece
    second_rows(wlhs, pool_pad, second)
    here = pl.ds(pl.multiple_of(8 * sy, 8), 8)
    outs = []
    for d in order:
        outs.append(remote(second.at[:, theirs(d), :], rows_out.at[here], os_.at[0], or_.at[0], peers[d - 1]))
    kept = pltpu.make_async_copy(second.at[:, mine, :], rows_out.at[here], ls.at[3])
    lines = lax.broadcasted_iota(jnp.int32, (16, 128), 0)

    def rounded(total, buffer):
        buffer[...] = total.astype(BF16)

        @pl.when(sx == 6)
        def _():
            fold_high, fold_low = split(jnp.sum(total[3][0:2], axis=0, keepdims=True))
            buffer[3] = jnp.where(lines == 0, fold_high.astype(F32), fold_low.astype(F32)).astype(BF16)

    settle(recv1.at[pl.ds(1, 7)], s1.at[0], r1.at[0])
    sum1 = pack1[pl.ds(4 * sx, 4)]
    for d in range(1, 8):
        sum1 = sum1 + recv1[d].astype(F32)
    rounded(sum1, half1)
    reduce1 = []
    for e in range(1, 16):
        reduce1.append(remote(half1, sums1.at[group1], t1.at[0], q1.at[0], mates1[e - 1]))
    for copy in reduce1:
        copy.start()
    sums1[group1] = half1[...]
    for copy in outs + [kept]:
        copy.start()
    settle(early2.at[pl.ds(1, 15)], s2.at[0], r2.at[0])
    settle(late2.at[pl.ds(1, 15)], s3.at[0], r3.at[0])
    here2 = pack2[pl.ds(3 * rep, 3), mine, :]
    there2 = pack2[pl.ds(6 + 5 * rep, 5), mine, :]
    for e in range(1, 16):
        here2 = here2 + early2[e].astype(F32)
        there2 = there2 + late2[e].astype(F32)
    for i in range(8):
        for h in range(2):
            part2[2 * i + h] = (here2[i] if i < 3 else there2[i - 3])[8 * h : 8 * h + 8]
    reduce2 = []
    for d in range(1, 8):
        rows = pl.ds(2 * (lax.rem(sx + d, 8)), 2)
        reduce2.append(remote(part2.at[rows], parts2.at[d], t2.at[0], q2.at[0], column[d - 1]))
    for copy in reduce2:
        copy.start()
    settle(parts2.at[pl.ds(1, 7)], t2.at[0], q2.at[0])
    own = pl.ds(2 * sx, 2)
    total2 = part2[own]
    for d in range(1, 8):
        total2 = total2 + parts2[d]
    whole2[rep, own] = total2
    gather2 = []
    for e in range(1, 16):
        gather2.append(
            remote(whole2.at[rep, own], whole2.at[rep, own], g2.at[0], h2.at[0], mates2[e - 1])
        )
    for copy in gather2:
        copy.start()
    settle(sums1.at[pl.ds(0, 15)], t1.at[0], q1.at[0])
    total1 = sums1[0].astype(F32)
    for m in range(1, 16):
        total1 = total1 + sums1[m].astype(F32)
    rounded(total1, last1)
    slots = pl.ds(4 * sx, 4)
    gather1 = []
    for d in range(1, 8):
        gather1.append(remote(last1, all1.at[slots], g1.at[0], h1.at[0], column[d - 1]))
    for copy in gather1:
        copy.start()
    all1[slots] = last1[...]
    kept.wait()
    settle(rows_out.at[pl.ds(0, 56)], os_.at[0], or_.at[0])
    settle(pack1.at[pl.ds(0, 15)], g2.at[0], h2.at[0])
    settle(all1.at[pl.ds(0, 28)], g1.at[0], h1.at[0])


def final_kernel(scale, rows, whole2, all1, b2, second_out, gw2_out, gb2_out, gw1_out, gb1_out):
    square = (16, 16)
    diagonal = lax.broadcasted_iota(jnp.int32, square, 0) == lax.broadcasted_iota(jnp.int32, square, 1)
    bias = jnp.sum(jnp.where(diagonal, b2[...], 0.0), axis=1, keepdims=True)
    second_out[...] = jnp.swapaxes(rows[...].astype(F32) + bias[None], 0, 1)
    def tap(plane, row, z):
        return 3 * (8 - 3 * plane - row) + z

    low = {0: (1, 0), 1: (1, 1), 2: (1, 2), 6: (0, 0), 7: (0, 1), 8: (0, 2), 9: (2, 0), 10: (2, 1), 11: (2, 2)}
    high = {3: ((1, 0), (1, 1)), 4: ((1, 2), None), 12: ((0, 0), (0, 1)), 13: ((0, 2), (2, 0)), 14: ((2, 1), (2, 2))}
    parts = []
    for half in range(2):
        for i in range(8):
            slot = 3 * half + i if i < 3 else 6 + 5 * half + i - 3
            for h in range(2):
                at = slice(8 * h, 8 * h + 8)
                tile = whole2[half, 2 * i + h] * scale
                if slot in low:
                    gw2_out[tap(*low[slot], 0), at, :] = tile[:, 0:64]
                    gw2_out[tap(*low[slot], 1), at, :] = tile[:, 64:128]
                elif slot in high:
                    one, other = high[slot]
                    gw2_out[tap(*one, 2), at, :] = tile[:, 0:64]
                    if other:
                        gw2_out[tap(*other, 2), at, :] = tile[:, 64:128]
                    else:
                        parts.append(tile[:, 64:65])
    gb2_out[...] = jnp.sum(jnp.where(diagonal, jnp.concatenate(parts, axis=0), 0.0), axis=0, keepdims=True)
    for i in range(27):
        block = all1[i].astype(F32) * scale
        for h in range(2):
            tile = block[8 * h : 8 * h + 8]
            if i < 18:
                at = 16 * i + 8 * h
                for z in range(2):
                    gw1_out[3 * (at // 32) + z, at % 32 : at % 32 + 8, :] = tile[:, 64 * z : 64 * z + 64]
            else:
                for z in range(2):
                    at = 144 * z + 16 * (i - 18) + 8 * h
                    gw1_out[3 * (at // 32) + 2, at % 32 : at % 32 + 8, :] = tile[:, 64 * z : 64 * z + 64]
    gb1_out[...] = jnp.sum(all1[27].astype(F32)[0:2, 64:128], axis=0, keepdims=True) * scale


def dma(n):
    return pltpu.SemaphoreType.DMA((n,))


def per_device(volume, first_kernel, first_bias, second_kernel, second_bias, cotangent):
    scale = 1.0 / math.sqrt(131072)
    k1 = first_kernel.transpose(2, 3, 4, 1, 0).reshape(27, 32, 64)
    k2 = second_kernel.transpose(2, 3, 4, 0, 1).reshape(27, 16, 64)
    outs = [((64, 16, 128), BF16), ((2, 16, 8, 128), F32), ((32, 16, 128), BF16)]
    scratch = [
        ((32, 2, 16, 256), BF16),
        ((16, 64, 128), BF16),
        ((27, 32, 64), BF16),
        ((1, 64), F32),
        ((27, 16, 64), BF16),
        ((2, 16, 32, 256), BF16),
        ((66, 16, 128), BF16),
        ((14, 16, 128), BF16),
        ((4, 18, 32, 256), BF16),
        ((3, 10, 128, 128), BF16),
        ((14, 128, 128), BF16),
        ((384, 576), BF16),
        ((384, 256), BF16),
        ((256, 384), BF16),
        ((192, 1152), BF16),
        ((1, 8, 64, 128), BF16),
        ((3, 10, 64, 128), BF16),
        ((2, 16, 64, 256), BF16),
        ((8, 128, 128), BF16),
        ((304, 256), F32),
        ((1152, 256), F32),
        ((32, 16, 128), F32),
        ((32, 16, 128), BF16),
        ((8, 4, 16, 128), BF16),
        ((4, 16, 128), BF16),
        ((16, 4, 16, 128), BF16),
        ((4, 16, 128), BF16),
        ((16, 128, 128), F32),
        ((16, 128, 128), BF16),
        ((16, 3, 16, 128), BF16),
        ((16, 5, 16, 128), BF16),
        ((16, 8, 128), F32),
        ((8, 2, 8, 128), F32),
    ]
    sems = [5, 4] + [1] * 2 + [8] * 2 + [2] * 2 + [1] * 22
    rows, whole2, all1 = pl.pallas_call(
        whole_kernel,
        out_shape=tuple(jax.ShapeDtypeStruct(s, t) for s, t in outs),
        in_specs=[pl.BlockSpec(memory_space=pl.ANY)] * 5,
        out_specs=tuple([VMEM] * 3),
        scratch_shapes=[pltpu.VMEM(s, t) for s, t in scratch] + [dma(n) for n in sems],
        compiler_params=pltpu.CompilerParams(
            vmem_limit_bytes=LIMIT, collective_id=0, has_side_effects=True
        ),
    )(volume[0], cotangent[0, :, 0], k1, first_bias[None], k2)
    finals = [((16, 64, 128), F32), ((27, 16, 64), F32), ((1, 16), F32), ((27, 32, 64), F32), ((1, 64), F32)]
    second_out, gw2, gb2, gw1, gb1 = pl.pallas_call(
        functools.partial(final_kernel, scale),
        out_shape=tuple(jax.ShapeDtypeStruct(s, t) for s, t in finals),
        in_specs=[VMEM] * 4,
        out_specs=tuple([VMEM] * 5),
        compiler_params=pltpu.CompilerParams(vmem_limit_bytes=LIMIT),
    )(rows, whole2, all1, second_bias[None])
    return (
        second_out[None, :, None],
        gw1.reshape(3, 3, 3, 32, 64).transpose(4, 3, 0, 1, 2),
        gb1[0],
        gw2.reshape(3, 3, 3, 16, 64).transpose(3, 4, 0, 1, 2),
        gb2[0],
    )


def solution(mesh):
    placed = (
        P("rep", None, "sx", "sy", None),
        P(),
        P(),
        P("sy", None, None, None, None),
        P("sy"),
        P("rep", "sy", "sx", None, None),
    )
    return jax.shard_map(
        per_device,
        mesh=mesh,
        in_specs=placed,
        out_specs=(
            P("rep", "sy", "sx", None, None),
            P(),
            P(),
            P("sy", None, None, None, None),
            P("sy"),
        ),
        check_vma=False,
    )
```
